128 devices in a mesh: space: 16 (over x, z_lo, core), sample: 8 (over y, z_hi).
Axes of the slice: x: 4, y: 4, z: 4 (z_hi: 2, z_lo: 2; z = z_hi * 2 + z_lo), core: 2. Of those that a mesh axis runs over, the one named last changes fastest.
Arguments:
- ensemble: bfloat16 [48, 8, 1024, 1024], P(None, 'sample', 'space'), may hold values from -6 to 6
- map_one: bfloat16 [1024, 256], P('space'), may hold values from -0.1875 to 0.1875
- map_two: bfloat16 [1024, 256], replicated, may hold values from -0.1875 to 0.1875
- map_three: bfloat16 [48, 256], replicated, may hold values from -0.875 to 0.875
- map_four: bfloat16 [8, 256], P('sample'), may hold values from -2 to 2
- core_one: bfloat16 [1024, 128], replicated, may hold values from -0.1875 to 0.1875
- core_two: bfloat16 [1024, 128], replicated, may hold values from -0.1875 to 0.1875
- core_three: bfloat16 [48, 128], replicated, may hold values from -0.875 to 0.875
- core_four: bfloat16 [8, 128], replicated, may hold values from -2 to 2
Outputs:
- sketch_one: float32 [1024, 256], P('space', 'sample')
- sketch_two: float32 [1024, 256], P(('space', 'sample'))
- sketch_three: float32 [48, 256], replicated
- sketch_four: float32 [8, 256], P('sample')
- core_sketch: float32 [128, 16384, 128], P(None, ('space', 'sample'))
The draws below stay inside these ranges and needn't reach their ends.
All inputs are finite; a program needn't handle non-finite values.
Results may differ from the reference program's by a relative error of at most 0.0029.
Values sent between devices are 32-bit elements; how exact they have to be, the bound alone decides.
A program may use at most 128 MiB of HBM per device.

```python
import jax
import jax.numpy as jnp
from jax import lax

N1 = 1024
N2 = 1024
K = 256
R = 128
TS = 16
SLABS = 3
TT = 48
NS = 8


def strengthened(entries, rng, source, target, shards_of, factor):
    owner, partner = [(jnp.arange(entries.shape[axis_at]) // (entries.shape[axis_at] // shards_of)).reshape([-1 if axis == axis_at else 1 for axis in range(entries.ndim)]) for axis_at in (source, target)]
    chosen = jax.random.permutation(rng, shards_of)[partner]
    strong = (owner == chosen) | (owner == (partner + shards_of // 2) % shards_of)
    return jnp.where(strong, factor * entries, entries)


def levels(key, dims, cuts, smallest, top_value):
    def one(position, parts):
        heights = jax.random.uniform(jax.random.fold_in(jax.random.fold_in(key, 6), position), (parts,), jnp.float32, smallest / len(cuts), top_value / len(cuts))
        return jnp.repeat(jnp.exp(heights), dims[position] // parts).reshape((-1,) + (1,) * (len(dims) - position - 1))

    gain = one(*cuts[0])
    for cut in cuts[1:]:
        gain = gain * one(*cut)
    return gain


def noise(rng, shape, spread, bound, shards=(), dtype=jnp.bfloat16):
    values = jax.random.normal(rng, shape, jnp.float32) * spread
    if len(shards) > 0:
        values = levels(rng, shape, shards, -0.22, 0.18) * values
    return jnp.clip(values, min=-bound, max=bound).astype(dtype)


def heavy_noise(key, extent, scale, most, split, heavy, dtype=jnp.bfloat16):
    entries = scale * jax.random.normal(key, extent, jnp.float32)
    if split:
        entries = entries * levels(key, extent, split, -0.22, 0.18)
    return jnp.clip(strengthened(entries, jax.random.fold_in(key, 3), *heavy), -most, most).astype(dtype)


def setup_inputs(seed: int = 0) -> dict:
    seeds = jax.random.split(jax.random.key(seed), 10)
    ensemble = heavy_noise(seeds[0], (TT, NS, N1, N2), 1.0, 6.0, ((1, 8), (2, 16)), (2, 3, 16, 2.0))
    map_one = noise(seeds[1], (N1, K), N1 ** -0.5, 0.1875, ((0, 16),))
    map_two = noise(seeds[2], (N2, K), N2 ** -0.5, 0.1875)
    map_three = noise(seeds[3], (TT, K), TT ** -0.5, 0.875)
    map_four = noise(seeds[4], (NS, K), NS ** -0.5, 2.0, ((0, 8),))
    core_one = noise(seeds[5], (N1, R), N1 ** -0.5, 0.1875)
    core_two = noise(seeds[6], (N2, R), N2 ** -0.5, 0.1875)
    core_three = noise(seeds[7], (TT, R), TT ** -0.5, 0.875)
    core_four = noise(seeds[8], (NS, R), NS ** -0.5, 2.0)
    return {"ensemble": ensemble, "map_one": map_one, "map_two": map_two, "map_three": map_three, "map_four": map_four, "core_one": core_one, "core_two": core_two, "core_three": core_three, "core_four": core_four}


def reference(ensemble, map_one, map_two, map_three, map_four, core_one, core_two, core_three, core_four):
    high = lax.Precision.HIGHEST
    joined = jnp.concatenate([map_two, core_two], axis=1)
    rows_one = map_one.astype(jnp.float32)
    rows_four = map_four.astype(jnp.float32)
    phi_one = core_one.astype(jnp.float32)
    phi_four = core_four.astype(jnp.float32)
    sketch_one = jnp.zeros((N1, K), jnp.float32)
    sketch_two = jnp.zeros((N2, K), jnp.float32)
    sketch_four = jnp.zeros((NS, K), jnp.float32)
    core = jnp.zeros((R, R, R, R), jnp.float32)
    thirds = []
    for index in range(SLABS):
        block = ensemble[index * TS:(index + 1) * TS]
        flat = block.reshape(-1, N2)
        both = jnp.dot(flat, joined, preferred_element_type=jnp.float32)
        proj = both[:, :K].reshape(TS, NS, N1, K)
        cproj = both[:, K:].reshape(TS, NS, N1, R)
        third = map_three[index * TS:(index + 1) * TS].astype(jnp.float32)
        time_core = core_three[index * TS:(index + 1) * TS].astype(jnp.float32)
        pair_ts = third[:, None, :] * rows_four[None, :, :]
        pair_si = rows_four[:, None, :] * rows_one[None, :, :]
        pair_ti = third[:, None, :] * rows_one[None, :, :]
        sketch_one = sketch_one + jnp.einsum('tsik,tsk->ik', proj, pair_ts, precision=high)
        thirds.append(jnp.einsum('tsik,sik->tk', proj, pair_si, precision=high))
        sketch_four = sketch_four + jnp.einsum('tsik,tik->sk', proj, pair_ti, precision=high)
        krao = (pair_ts[:, :, None, :] * rows_one[None, None, :, :]).astype(jnp.bfloat16).reshape(-1, K)
        sketch_two = sketch_two + jnp.dot(flat.T, krao, preferred_element_type=jnp.float32)
        half = jnp.einsum('tsib,ia->tsab', cproj, phi_one, precision=high)
        quarter = jnp.einsum('tsab,sd->tdab', half, phi_four, precision=high)
        core = core + jnp.einsum('tdab,tc->abcd', quarter, time_core, precision=high)
    sketch_three = jnp.concatenate(thirds, axis=0)
    return sketch_one, sketch_two, sketch_three, sketch_four, core.reshape(R, R * R, R)
```

```python
import jax
import jax.numpy as jnp
from jax import lax
from jax.experimental import pallas as pl
from jax.experimental.pallas import tpu as pltpu
from jax.sharding import PartitionSpec as P

F32 = jnp.float32
BF16 = jnp.bfloat16
MESH = pl.DeviceIdType.MESH
T = 8


def two_terms(value):
    high = value.astype(BF16)
    low = (value - high.astype(F32)).astype(BF16)
    return high, low


def local_kernel(x_ref, one_ref, two_ref, three_ref, four_ref, ctwo_ref, cp_ref, q_ref, s1_ref, s2_ref, acc_one):
    step = pl.program_id(0)
    points = x_ref.shape[2]
    x = x_ref[...].reshape(T * points, x_ref.shape[3])
    one = one_ref[...].astype(F32)
    four = four_ref[...].astype(F32)
    third = three_ref[pl.ds(pl.multiple_of(step * T, T), T), :]

    cproj = jnp.dot(x, ctwo_ref[...], preferred_element_type=F32)
    for pair in range(T // 2):
        tile = cproj[pair * 128 : (pair + 1) * 128].T.reshape(8, 2, 8, 128)
        for core in range(2):
            cp_ref[core, :, :, pair * 128 : (pair + 1) * 128] = tile[:, core]

    proj = jnp.dot(x, two_ref[...], preferred_element_type=F32).reshape(T, points, 256)
    q = jnp.sum(proj * one[None], axis=1)
    q_ref[0] = q[:, :128]
    q_ref[1] = q[:, 128:]
    first = jnp.sum(proj * third[:, None, :], axis=0)
    krao = ((third * four)[:, None, :] * one[None]).astype(BF16).reshape(T * points, 256)
    second = lax.dot_general(x, krao, (((0,), (0,)), ((), ())), preferred_element_type=F32)

    @pl.when(step == 0)
    def _():
        acc_one[...] = first
        s2_ref[...] = second

    @pl.when(step > 0)
    def _():
        acc_one[...] += first
        s2_ref[...] += second

    @pl.when(step == pl.num_programs(0) - 1)
    def _():
        s1_ref[...] = jnp.zeros_like(s1_ref)
        s1_ref[:, :points] = (acc_one[...] * four).T


def local_sketches(ensemble, map_one, map_two, map_three, map_four, core_two):
    steps = ensemble.shape[0] // T
    whole = lambda shape: pl.BlockSpec(shape, lambda i: (0,) * len(shape))
    return pl.pallas_call(
        local_kernel,
        grid=(steps,),
        in_specs=[
            pl.BlockSpec((T, 1, 64, 1024), lambda i: (i, 0, 0, 0)),
            whole((64, 256)),
            whole((1024, 256)),
            whole((48, 256)),
            whole((1, 256)),
            whole((1024, 128)),
        ],
        out_specs=[
            pl.BlockSpec((2, 8, 8, T * 64), lambda i: (0, 0, 0, i)),
            pl.BlockSpec((2, T, 128), lambda i: (0, i, 0)),
            whole((256, 128)),
            whole((1024, 256)),
        ],
        out_shape=[
            jax.ShapeDtypeStruct((2, 8, 8, 3072), F32),
            jax.ShapeDtypeStruct((2, 48, 128), F32),
            jax.ShapeDtypeStruct((256, 128), F32),
            jax.ShapeDtypeStruct((1024, 256), F32),
        ],
        scratch_shapes=[pltpu.VMEM((64, 256), F32)],
        compiler_params=pltpu.CompilerParams(dimension_semantics=("arbitrary",)),
        name="local_sketches",
    )(ensemble, map_one, map_two, map_three.astype(F32), map_four, core_two)


CHUNKS = 6
S_CORE, S_A, S_B, S_C, S_D, S_E = 0, 6, 12, 18, 24, 30
S_SAMPLE = 36
S_ONE = S_SAMPLE + 7 * CHUNKS
S_Q = S_ONE + 7
S_TWO = S_Q + 14
S_ALL = S_TWO + 12


def exchange_kernel(
    cp_ref, q_ref, s1_ref, s2_ref, cone_ref, three_ref, four_ref,
    h_ref, o1_ref, o2_ref, o3_ref, o4_ref,
    weight, cp_in, half, xa, xb, xr, za, zr, zs, zb, zc, fin, parts,
    q_in, q_x, q_z, q_s, q_o, q_oi, s1_in, s2_in, s2_y, s2_h, s2_r, s2_v, s2_x, s2_xs, s2_z, s2_zs, s2_w,
    send_sem, recv_sem,
):
    space = lax.axis_index("space")
    sample = lax.axis_index("sample")
    x, zl, c = space // 4, (space // 2) % 2, space % 2
    y, zh = sample // 2, sample % 2
    at_x = lambda p: (p * 4 + zl * 2 + c, sample)
    xs = [lax.rem(x + d, 4) for d in range(4)]
    mate = (x * 4 + zl * 2 + (1 - c), sample)
    zmate = (x * 4 + (1 - zl) * 2 + c, sample)
    right, left = at_x(xs[1]), at_x(xs[3])
    samples = [lax.rem(sample + d, 8) for d in range(8)]
    ys = [lax.rem(y + d, 4) for d in range(4)]
    up, down = (space, ys[1] * 2 + zh), (space, ys[3] * 2 + zh)
    hmate = (space, y * 2 + 1 - zh)

    barrier = pltpu.get_barrier_semaphore()
    peers = [mate, zmate] + [at_x(xs[d]) for d in range(1, 4)] + [(space, samples[d]) for d in range(1, 8)]
    for peer in peers:
        pl.semaphore_signal(barrier, inc=1, device_id=peer, device_id_type=MESH)
    pl.semaphore_wait(barrier, len(peers))

    copies = []

    def send(src, dst, slot, to):
        copy = pltpu.make_async_remote_copy(
            src_ref=src, dst_ref=dst, send_sem=send_sem.at[slot], recv_sem=recv_sem.at[slot],
            device_id=to, device_id_type=MESH,
        )
        copy.start()
        copies.append(copy)
        return copy

    core_copies = []
    for n in range(CHUNKS):
        lanes = pl.ds(n * T * 64, T * 64)
        core_copies.append(send(cp_ref.at[1 - c, :, :, lanes], cp_in.at[:, :, lanes], S_CORE + n, mate))
    q_copy = send(q_ref.at[1 - c], q_in, S_Q, mate)
    s2_copy = send(s2_ref.at[:, 1 - c], s2_in, S_TWO, mate)
    one_copies = []
    for d in range(1, 8):
        rows = pl.ds(pl.multiple_of(samples[d] * 32, 32), 32)
        one_copies.append(send(s1_ref.at[rows], s1_in.at[d - 1], S_ONE + d - 1, (space, samples[d])))

    own = cone_ref[pl.ds(pl.multiple_of(space * 64, 64), 64), :]
    other = cone_ref[pl.ds(pl.multiple_of((x * 4 + zl * 2 + 1 - c) * 64, 64), 64), :]
    weight[...] = jnp.zeros_like(weight)
    weight[0:64, 0:128] = own
    weight[64:128, 128:256] = own
    weight[128:192, 0:128] = other
    weight[192:256, 128:256] = other

    far = xs[2]
    first_stage = []
    for n in range(CHUNKS):
        core_copies[n].wait_recv()
        rows = []
        for p in range(T // 2):
            lanes = pl.ds(n * T * 64 + p * 128, 128)
            mine = cp_ref[c, :, :, lanes].reshape(64, 128)
            theirs = cp_in[:, :, lanes].reshape(64, 128)
            rows.append(jnp.concatenate([mine, theirs], axis=1))
        high, low = two_terms(jnp.concatenate(rows, axis=0))
        res = jnp.dot(high, weight[...], preferred_element_type=F32)
        res = res + jnp.dot(low, weight[...], preferred_element_type=F32)
        for p in range(T // 2):
            for e in range(2):
                half[n, p * 2 + e] = res[p * 64 : (p + 1) * 64, e * 128 : (e + 1) * 128].reshape(4, 2, 8, 128)
        if n % 2 == 0:
            k = n // 2
            first_stage.append((
                send(half.at[n, :, far, 0], xa.at[k, 0], S_A + n, right),
                send(half.at[n, :, far, 1], xa.at[k, 1], S_B + n, left),
            ))
        else:
            first_stage.append((send(half.at[n, :, :, 1 - zl], za.at[n // 2], S_A + n, zmate),))

    q_copy.wait_recv()
    q_in[...] += q_ref[c]
    q_copies = [send(q_in, q_x.at[d - 1], S_Q + d, at_x(xs[d])) for d in range(1, 4)]

    s2_copy.wait_recv()
    s2_in[...] += s2_ref[:, c]
    yfar = ys[2]
    y_up = send(s2_in.at[pl.ds(0, 4), yfar], s2_y.at[0], S_TWO + 1, up)
    y_down = send(s2_in.at[pl.ds(4, 4), yfar], s2_y.at[1], S_TWO + 2, down)

    second_stage = []
    for n in range(CHUNKS):
        for copy in first_stage[n]:
            copy.wait_recv()
        k = n // 2
        if n % 2 == 0:
            half[n, :, xs[1], 0] += xa[k, 0]
            half[n, :, xs[3], 1] += xa[k, 1]
            second_stage.append((
                send(half.at[n, :, xs[1]], xb.at[k, 0], S_C + n, right),
                send(half.at[n, :, xs[3]], xb.at[k, 1], S_D + n, left),
            ))
        else:
            zr[k] = half[n, :, :, zl] + za[k]
            second_stage.append((
                send(zr.at[k, pl.ds(0, T // 2), far], zb.at[k, 0], S_B + n, right),
                send(zr.at[k, pl.ds(T // 2, T // 2), far], zb.at[k, 1], S_C + n, left),
            ))

    for copy in q_copies:
        copy.wait_recv()
    q_z[0] = q_in[...] + q_x[0] + q_x[1] + q_x[2]
    q_copy = send(q_z.at[0], q_z.at[1], S_Q + 4, zmate)

    y_up.wait_recv()
    s2_in[pl.ds(0, 4), ys[1]] += s2_y[0]
    y_down.wait_recv()
    s2_in[pl.ds(4, 4), ys[3]] += s2_y[1]
    y_up = send(s2_in.at[:, ys[1]], s2_h.at[0], S_TWO + 3, up)
    y_down = send(s2_in.at[:, ys[3]], s2_h.at[1], S_TWO + 4, down)

    third_stage = []
    for n in range(CHUNKS):
        for copy in second_stage[n]:
            copy.wait_recv()
        k = n // 2
        if n % 2 == 0:
            xr[k] = half[n, :, x] + xb[k, 0] + xb[k, 1]
            third_stage.append((send(xr.at[k, :, 1 - zl], zs.at[k], S_E + n, zmate),))
        else:
            zr[k, pl.ds(0, T // 2), xs[1]] += zb[k, 0]
            zr[k, pl.ds(T // 2, T // 2), xs[3]] += zb[k, 1]
            third_stage.append((
                send(zr.at[k, :, xs[1]], zc.at[k, 0], S_D + n, right),
                send(zr.at[k, :, xs[3]], zc.at[k, 1], S_E + n, left),
            ))

    q_copy.wait_recv()
    total = q_z[0] + q_z[1]
    mine3 = jnp.where(c == 0, three_ref[:, :128], three_ref[:, 128:])
    mine4 = jnp.where(c == 0, four_ref[:, :128], four_ref[:, 128:]).astype(F32)
    fourth = jnp.sum(total * mine3, axis=0, keepdims=True)
    q_s[0] = total * mine4
    q_copies = [send(q_s.at[0], q_s.at[d], S_Q + 4 + d, (space, samples[d])) for d in range(1, 8)]

    y_up.wait_recv()
    y_down.wait_recv()
    s2_r[...] = s2_in[:, y] + s2_h[0] + s2_h[1]
    x_copies = []
    for d in range(1, 4):
        x_copies.append(send(s2_r.at[pl.ds(xs[d] * 2, 2)], s2_x.at[d - 1], S_TWO + 4 + d, at_x(xs[d])))

    sample_copies = []
    for n in range(CHUNKS):
        for copy in third_stage[n]:
            copy.wait_recv()
        k = n // 2
        if n % 2 == 0:
            value = xr[k, :, zl] + zs[k]
        else:
            value = zr[k, :, x] + zc[k, 0] + zc[k, 1]
        fin[n] = value.reshape(T * 8, 128)
        for s in range(8):
            parts[n, s] = fin[n, pl.ds(s, T, stride=8), :]
        h_ref[sample, pl.ds(n * T, T)] = parts[n, sample]
        for d in range(1, 8):
            sample_copies.append(send(
                parts.at[n, samples[d]], h_ref.at[sample, pl.ds(n * T, T)],
                S_SAMPLE + 7 * n + d - 1, (space, samples[d]),
            ))

    for copy in x_copies:
        copy.wait_recv()
    s2_xs[...] = s2_r[pl.ds(x * 2, 2)] + s2_x[0] + s2_x[1] + s2_x[2]
    s2_copy = send(s2_xs.at[1 - zl], s2_z, S_TWO + 8, zmate)

    for copy in q_copies:
        copy.wait_recv()
    total = q_s[0]
    for d in range(1, 8):
        total = total + q_s[d]
    q_o[pl.ds(0, 48)] = total
    q_o[pl.ds(48, 8)] = jnp.broadcast_to(fourth, (8, 128))
    q_copy = send(q_o, q_oi, S_Q + 12, mate)

    s2_copy.wait_recv()
    s2_zs[...] = (s2_xs[zl] + s2_z[...]).reshape(2, 8, 256)
    s2_copy = send(s2_zs.at[1 - zh], s2_w, S_TWO + 9, hmate)

    for copy in one_copies:
        copy.wait_recv()
    total = s1_ref[pl.ds(pl.multiple_of(sample * 32, 32), 32)]
    for d in range(1, 8):
        total = total + s1_in[d - 1]
    o1_ref[...] = total

    q_copy.wait_recv()
    here, there = q_o[...], q_oi[...]
    low = jnp.where(c == 0, here, there)
    top = jnp.where(c == 0, there, here)
    o3_ref[:, :128] = low[:48]
    o3_ref[:, 128:] = top[:48]
    o4_ref[:, :128] = low[48:56]
    o4_ref[:, 128:] = top[48:56]

    s2_copy.wait_recv()
    o2_ref[...] = s2_zs[zh] + s2_w[...]
    for copy in sample_copies:
        copy.wait_recv()
    for copy in copies:
        copy.wait_send()


def exchange(cp, q, s1, s2, core_one, map_three, map_four):
    k = CHUNKS // 2
    vmem = lambda *shape: pltpu.VMEM(shape, F32)
    return pl.pallas_call(
        exchange_kernel,
        in_specs=[pl.BlockSpec(memory_space=pltpu.VMEM)] * 7,
        out_specs=[pl.BlockSpec(memory_space=pltpu.VMEM)] * 5,
        out_shape=[
            jax.ShapeDtypeStruct((8, 48, 128), F32),
            jax.ShapeDtypeStruct((32, 128), F32),
            jax.ShapeDtypeStruct((8, 256), F32),
            jax.ShapeDtypeStruct((48, 256), F32),
            jax.ShapeDtypeStruct((8, 256), F32),
        ],
        scratch_shapes=[
            pltpu.VMEM((256, 256), BF16),
            vmem(8, 8, 3072),
            vmem(CHUNKS, T, 4, 2, 8, 128),
            vmem(k, 2, T, 8, 128),
            vmem(k, 2, T, 2, 8, 128),
            vmem(k, T, 2, 8, 128),
            vmem(k, T, 4, 8, 128),
            vmem(k, T, 4, 8, 128),
            vmem(k, T, 8, 128),
            vmem(k, 2, T // 2, 8, 128),
            vmem(k, 2, T, 8, 128),
            vmem(CHUNKS, T * 8, 128),
            vmem(CHUNKS, 8, T, 128),
            vmem(48, 128),
            vmem(3, 48, 128),
            vmem(2, 48, 128),
            vmem(8, 48, 128),
            vmem(56, 128),
            vmem(56, 128),
            vmem(7, 32, 128),
            vmem(8, 4, 16, 256),
            vmem(2, 4, 16, 256),
            vmem(2, 8, 16, 256),
            vmem(8, 16, 256),
            vmem(8, 128),
            vmem(3, 2, 16, 256),
            vmem(2, 16, 256),
            vmem(16, 256),
            vmem(2, 8, 256),
            vmem(8, 256),
            pltpu.SemaphoreType.DMA((S_ALL,)),
            pltpu.SemaphoreType.DMA((S_ALL,)),
        ],
        compiler_params=pltpu.CompilerParams(collective_id=0, has_side_effects=True),
        name="exchange",
    )(cp, q, s1, s2.reshape(8, 2, 4, 16, 256), core_one, map_three.astype(F32), map_four)


def final_kernel(h_ref, three_ref, four_ref, i1_ref, i2_ref, i3_ref, i4_ref, out_ref, o1_ref, o2_ref, o3_ref, o4_ref, grown, blocks):
    step = pl.program_id(0)

    @pl.when(step == 0)
    def _():
        three = three_ref[...]
        three = jnp.concatenate([three, three], axis=0)
        for s in range(8):
            high, low = two_terms(h_ref[s])
            both = jnp.concatenate([high, low], axis=0)
            grown[pl.ds(s, 128, stride=8), :] = lax.dot_general(
                both, three, (((0,), (0,)), ((), ())), preferred_element_type=F32
            )
        four = jnp.tile(four_ref[...].astype(F32), (16, 2))
        row = lax.broadcasted_iota(jnp.int32, (128, 256), 0) // 8
        col = lax.broadcasted_iota(jnp.int32, (128, 256), 1) // 128
        for j in range(8):
            block = jnp.where(row == col + 2 * j, four, 0.0).astype(BF16)
            blocks[j, 0:128] = block
            blocks[j, 128:256] = block
        o1_ref[...] = i1_ref[...].T[:64]
        o2_ref[...] = i2_ref[...]
        o3_ref[...] = i3_ref[...]
        o4_ref[...] = i4_ref[0:1]

    tile = grown[pl.ds(pl.multiple_of(step * 128, 128), 128), :].T
    high, low = two_terms(tile)
    both = jnp.concatenate([high, low], axis=1)
    for j in range(8):
        res = jnp.dot(both, blocks[j], preferred_element_type=F32)
        out_ref[2 * j] = res[:, :128]
        out_ref[2 * j + 1] = res[:, 128:]


def final(h, core_three, core_four, s1, s2, s3, s4):
    whole = lambda shape: pl.BlockSpec(shape, lambda i: (0,) * len(shape))
    return pl.pallas_call(
        final_kernel,
        grid=(8,),
        in_specs=[whole(a.shape) for a in (h, core_three, core_four, s1, s2, s3, s4)],
        out_specs=[
            pl.BlockSpec((16, 128, 128), lambda i: (i, 0, 0)),
            whole((64, 32)),
            whole((8, 256)),
            whole((48, 256)),
            whole((1, 256)),
        ],
        out_shape=[
            jax.ShapeDtypeStruct((128, 128, 128), F32),
            jax.ShapeDtypeStruct((64, 32), F32),
            jax.ShapeDtypeStruct((8, 256), F32),
            jax.ShapeDtypeStruct((48, 256), F32),
            jax.ShapeDtypeStruct((1, 256), F32),
        ],
        scratch_shapes=[pltpu.VMEM((1024, 128), F32), pltpu.VMEM((8, 256, 256), BF16)],
        compiler_params=pltpu.CompilerParams(dimension_semantics=("arbitrary",)),
        name="final",
    )(h, core_three, core_four, s1, s2, s3, s4)


def on_device(
    ensemble, map_one, map_two, map_three, map_four, core_one, core_two, core_three, core_four
):
    cp, q, s1, s2 = local_sketches(ensemble, map_one, map_two, map_three, map_four, core_two)
    h, s1, s2, s3, s4 = exchange(cp, q, s1, s2, core_one, map_three, map_four)
    core, s1, s2, s3, s4 = final(h, core_three, core_four, s1, s2, s3, s4)
    return (s1, s2, s3, s4, core)


def solution(mesh):
    placed = (
        P(None, "sample", "space", None),
        P("space", None),
        P(),
        P(),
        P("sample", None),
        P(),
        P(),
        P(),
        P(),
    )
    return jax.shard_map(
        on_device,
        mesh=mesh,
        in_specs=placed,
        out_specs=(
            P("space", "sample"),
            P(("space", "sample"), None),
            P(),
            P("sample", None),
            P(None, ("space", "sample"), None),
        ),
        check_vma=False,
    )
```

```python
import jax
import jax.numpy as jnp
from jax import lax
from jax.experimental import pallas as pl
from jax.experimental.pallas import tpu as pltpu
from jax.sharding import PartitionSpec as P

F32 = jnp.float32
BF16 = jnp.bfloat16
MESH = pl.DeviceIdType.MESH
T = 8


def two_terms(value):
    high = value.astype(BF16)
    low = (value - high.astype(F32)).astype(BF16)
    return high, low


CHUNKS = 6
KINDS = "zxzxzx"


def fused_kernel(
    ens_ref, two_ref, ctwo_ref, cone_ref, one_ref, three_ref, four_ref,
    h_ref, o1_ref, o2_ref, o3_ref, o4_ref,
    xv, two, ctwo, cone, krao, cp, weight, cp_in, half, xa, xb, xr, za, zr, zs, zb, zc, fin, parts,
    q_own, q_in, q_x, q_s, q_o, q_oi, s1_own, s1_in,
    s2, s2_in, s2_y, s2_h, s2_r, s2_x, s2_xs, s2_z,
    load_sem, send_sem, recv_sem,
):
    space = lax.axis_index("space")
    sample = lax.axis_index("sample")
    x, zl, c = space // 4, (space // 2) % 2, space % 2
    y, zh = sample // 2, sample % 2
    xs = [lax.rem(x + d, 4) for d in range(4)]
    ys = [lax.rem(y + d, 4) for d in range(4)]
    samples = [lax.rem(sample + d, 8) for d in range(8)]
    at = lambda px, pz: (px * 4 + pz * 2 + c, sample)
    mate = (x * 4 + zl * 2 + (1 - c), sample)
    zmate = at(x, 1 - zl)
    right, left = at(xs[1], zl), at(xs[3], zl)
    up, down = (space, ys[1] * 2 + zh), (space, ys[3] * 2 + zh)
    hmate = (space, y * 2 + 1 - zh)
    dmate = (x * 4 + (1 - zl) * 2 + c, y * 2 + 1 - zh)
    planes = [at(xs[d % 4], zl if d < 4 else 1 - zl) for d in range(8)]
    mates = [(space, samples[d]) for d in range(8)]

    barrier = pltpu.get_barrier_semaphore()
    peers = [mate, dmate] + planes[1:] + mates[1:]
    for peer in peers:
        pl.semaphore_signal(barrier, inc=1, device_id=peer, device_id_type=MESH)

    def load(src, dst, slot):
        copy = pltpu.make_async_copy(src, dst, load_sem.at[slot])
        copy.start()
        return copy

    load_ctwo = load(ctwo_ref, ctwo, CHUNKS)
    loads = [load(ens_ref.at[pl.ds(n * T, T), 0], xv.at[pl.ds(n * T, T)], n) for n in range(CHUNKS)]
    load_cone = load(cone_ref, cone, CHUNKS + 1)
    load_two = load(two_ref, two, CHUNKS + 2)

    copies = []

    def send(src, dst, to):
        slot = len(copies)
        copy = pltpu.make_async_remote_copy(
            src_ref=src, dst_ref=dst, send_sem=send_sem.at[slot], recv_sem=recv_sem.at[slot],
            device_id=to, device_id_type=MESH,
        )
        copy.start()
        copies.append(copy)
        return copy

    def arrived(group):
        for copy in group:
            copy.wait_recv()

    one = one_ref[...].astype(F32)
    four = four_ref[...].astype(F32)
    far, yfar = xs[2], ys[2]
    rows_in = T * 64
    core, st1, st2, st3, st4 = {}, {}, {}, {}, {}

    def project(n):
        loads[n].wait()
        block = xv[pl.ds(n * T, T)].reshape(rows_in, 1024)
        value = lax.dot_general(
            ctwo[...], block, (((0,), (1,)), ((), ())), preferred_element_type=F32
        ).reshape(8, 2, 8, rows_in)
        lanes = pl.ds(n * rows_in, rows_in)
        for e in range(2):
            cp[e, :, :, lanes] = value[:, e]
        if n == 0:
            pl.semaphore_wait(barrier, len(peers))
        core[n] = [send(cp.at[1 - c, :, :, lanes], cp_in.at[:, :, lanes], mate)]
        third = three_ref[n * T : (n + 1) * T, :].astype(F32)
        krao[n * rows_in : (n + 1) * rows_in, :] = (
            ((third * four)[:, None, :] * one[None]).astype(BF16).reshape(rows_in, 256)
        )

    def contract(n):
        arrived(core[n])
        rows = []
        for p in range(T // 2):
            lanes = pl.ds(n * rows_in + p * 128, 128)
            mine = cp[c, :, :, lanes].reshape(64, 128)
            theirs = cp_in[:, :, lanes].reshape(64, 128)
            rows.append(jnp.concatenate([mine, theirs], axis=1))
        high, low = two_terms(jnp.concatenate(rows, axis=0))
        res = jnp.dot(high, weight[...], preferred_element_type=F32)
        res = res + jnp.dot(low, weight[...], preferred_element_type=F32)
        for p in range(T // 2):
            for e in range(2):
                half[n, p * 2 + e] = res[p * 64 : (p + 1) * 64, e * 128 : (e + 1) * 128].reshape(4, 2, 8, 128)
        k = n // 2
        if KINDS[n] == "x":
            st1[n] = [send(half.at[n, :, far, 0], xa.at[k, 0], right), send(half.at[n, :, far, 1], xa.at[k, 1], left)]
        else:
            st1[n] = [send(half.at[n, :, :, 1 - zl], za.at[k], zmate)]

    def stage_two(n):
        arrived(st1[n])
        k = n // 2
        if KINDS[n] == "x":
            half[n, :, xs[1], 0] += xa[k, 0]
            half[n, :, xs[3], 1] += xa[k, 1]
            st2[n] = [send(half.at[n, :, xs[1]], xb.at[k, 0], right), send(half.at[n, :, xs[3]], xb.at[k, 1], left)]
        else:
            zr[k] = half[n, :, :, zl] + za[k]
            st2[n] = [
                send(zr.at[k, pl.ds(0, T // 2), far], zb.at[k, 0], right),
                send(zr.at[k, pl.ds(T // 2, T // 2), far], zb.at[k, 1], left),
            ]

    def stage_three(n):
        arrived(st2[n])
        k = n // 2
        if KINDS[n] == "x":
            xr[k] = half[n, :, x] + xb[k, 0] + xb[k, 1]
            st3[n] = [send(xr.at[k, :, 1 - zl], zs.at[k], zmate)]
        else:
            zr[k, pl.ds(0, T // 2), xs[1]] += zb[k, 0]
            zr[k, pl.ds(T // 2, T // 2), xs[3]] += zb[k, 1]
            st3[n] = [send(zr.at[k, :, xs[1]], zc.at[k, 0], right), send(zr.at[k, :, xs[3]], zc.at[k, 1], left)]

    def stage_four(n):
        arrived(st3[n])
        k = n // 2
        if KINDS[n] == "x":
            value = xr[k, :, zl] + zs[k]
        else:
            value = zr[k, :, x] + zc[k, 0] + zc[k, 1]
        fin[n] = value.reshape(T * 8, 128)
        for s in range(8):
            parts[n, s] = fin[n, pl.ds(s, T, stride=8), :]
        h_ref[sample, pl.ds(n * T, T)] = parts[n, sample]
        st4[n] = [
            send(parts.at[n, samples[d]], h_ref.at[sample, pl.ds(n * T, T)], mates[d]) for d in range(7, 0, -1)
        ]

    for n in range(CHUNKS):
        if n == 2:
            load_cone.wait()
            own = cone[pl.ds(pl.multiple_of(space * 64, 64), 64), :]
            other = cone[pl.ds(pl.multiple_of((x * 4 + zl * 2 + 1 - c) * 64, 64), 64), :]
            weight[...] = jnp.zeros_like(weight)
            weight[0:64, 0:128] = own
            weight[64:128, 128:256] = own
            weight[128:192, 0:128] = other
            weight[192:256, 128:256] = other
        if n == 0:
            load_ctwo.wait()
        project(n)
        if n >= 2:
            contract(n - 2)
    contract(CHUNKS - 2)
    contract(CHUNKS - 1)

    s2_core = []
    for b in range(4):
        s2[b] = lax.dot_general(
            xv[:, :, b * 256 : (b + 1) * 256].reshape(48 * 64, 256), krao[...],
            (((0,), (0,)), ((), ())), preferred_element_type=F32,
        ).reshape(2, 2, 4, 16, 256)
        s2_core.append(send(s2.at[b, :, 1 - c], s2_in.at[b], mate))

    load_two.wait()
    first = jnp.zeros((64, 256), F32)
    for n in range(CHUNKS):
        block = xv[pl.ds(n * T, T)].reshape(rows_in, 1024)
        third = three_ref[n * T : (n + 1) * T, :].astype(F32)
        proj = jnp.dot(block, two[...], preferred_element_type=F32).reshape(T, 64, 256)
        q = jnp.sum(proj * one[None], axis=1)
        q_own[0, pl.ds(n * T, T)] = q[:, :128]
        q_own[1, pl.ds(n * T, T)] = q[:, 128:]
        first = first + jnp.sum(proj * third[:, None, :], axis=0)
    q_core = send(q_own.at[1 - c], q_in, mate)
    s1_own[...] = jnp.zeros_like(s1_own)
    s1_own[:, :64] = (first * four).T
    s1_sends = []
    for d in range(1, 8):
        rows = pl.ds(pl.multiple_of(samples[d] * 32, 32), 32)
        s1_sends.append(send(s1_own.at[rows], s1_in.at[d - 1], mates[d]))

    stage_two(1)
    s2_one = []
    for b in range(4):
        s2_core[b].wait_recv()
        s2_in[b] += s2[b, :, c]
        s2_one.append((
            send(s2_in.at[b, 0, yfar], s2_y.at[b, 0], up),
            send(s2_in.at[b, 1, yfar], s2_y.at[b, 1], down),
        ))
    q_core.wait_recv()
    q_in[...] += q_own[c]
    q_space = [send(q_in, q_x.at[d - 1], planes[d]) for d in range(1, 8)]
    stage_two(0)
    stage_two(3)
    stage_two(5)
    s2_two = []
    for b in range(4):
        arrived(s2_one[b])
        s2_in[b, 0, ys[1]] += s2_y[b, 0]
        s2_in[b, 1, ys[3]] += s2_y[b, 1]
        s2_two.append((
            send(s2_in.at[b, :, ys[1]], s2_h.at[b, 0], up),
            send(s2_in.at[b, :, ys[3]], s2_h.at[b, 1], down),
        ))
    stage_two(2)
    stage_three(1)

    arrived(q_space)
    total = q_in[...]
    for d in range(1, 8):
        total = total + q_x[d - 1]
    mine3 = jnp.where(c == 0, three_ref[:, :128], three_ref[:, 128:]).astype(F32)
    mine4 = jnp.where(c == 0, four[:, :128], four[:, 128:])
    fourth = jnp.sum(total * mine3, axis=0, keepdims=True)
    q_s[0] = total * mine4
    q_sends = [send(q_s.at[0], q_s.at[d], mates[d]) for d in range(1, 8)]

    stage_three(0)
    stage_three(3)
    for b in range(4):
        arrived(s2_two[b])
        s2_r[b] = s2_in[b, :, y] + s2_h[b, 0] + s2_h[b, 1]
    s2_three = [send(s2_r.at[xs[d]], s2_x.at[d - 1], at(xs[d], zl)) for d in range(1, 4)]
    stage_three(5)
    stage_two(4)
    stage_three(2)
    stage_four(1)
    stage_four(0)
    stage_four(3)
    arrived(s2_three)
    s2_xs[...] = (s2_r[x] + s2_x[0] + s2_x[1] + s2_x[2]).reshape(2, 2, 8, 256)
    s2_four = [
        send(s2_xs.at[1 - zl, zh], s2_z.at[0], zmate),
        send(s2_xs.at[zl, 1 - zh], s2_z.at[1], hmate),
        send(s2_xs.at[1 - zl, 1 - zh], s2_z.at[2], dmate),
    ]
    stage_three(4)
    arrived(q_sends)
    total = q_s[0]
    for d in range(1, 8):
        total = total + q_s[d]
    q_o[pl.ds(0, 48)] = total
    q_o[pl.ds(48, 8)] = jnp.broadcast_to(fourth, (8, 128))
    q_last = send(q_o, q_oi, mate)
    stage_four(5)
    stage_four(2)
    stage_four(4)

    arrived(s1_sends)
    total = s1_own[pl.ds(pl.multiple_of(sample * 32, 32), 32)]
    for d in range(1, 8):
        total = total + s1_in[d - 1]
    o1_ref[...] = total[:, :64]

    q_last.wait_recv()
    here, there = q_o[...], q_oi[...]
    low = jnp.where(c == 0, here, there)
    top = jnp.where(c == 0, there, here)
    o3_ref[:, :128] = low[:48]
    o3_ref[:, 128:] = top[:48]
    o4_ref[:, :128] = low[48:56]
    o4_ref[:, 128:] = top[48:56]

    arrived(s2_four)
    o2_ref[...] = s2_xs[zl, zh] + s2_z[0] + s2_z[1] + s2_z[2]
    for n in range(CHUNKS):
        arrived(st4[n])
    for copy in copies:
        copy.wait_send()


def fused(ensemble, map_one, map_two, map_three, map_four, core_one, core_two):
    k = CHUNKS // 2
    vmem = lambda *shape: pltpu.VMEM(shape, F32)
    here = pl.BlockSpec(memory_space=pltpu.VMEM)
    there = pl.BlockSpec(memory_space=pl.ANY)
    slots = CHUNKS * 13 + 26 + 16 + 7
    return pl.pallas_call(
        fused_kernel,
        in_specs=[there] * 4 + [here] * 3,
        out_specs=[here] * 5,
        out_shape=[
            jax.ShapeDtypeStruct((8, 48, 128), F32),
            jax.ShapeDtypeStruct((32, 64), F32),
            jax.ShapeDtypeStruct((8, 256), F32),
            jax.ShapeDtypeStruct((48, 256), F32),
            jax.ShapeDtypeStruct((8, 256), F32),
        ],
        scratch_shapes=[
            pltpu.VMEM((48, 64, 1024), BF16),
            pltpu.VMEM((1024, 256), BF16),
            pltpu.VMEM((1024, 128), BF16),
            pltpu.VMEM((1024, 128), BF16),
            pltpu.VMEM((48 * 64, 256), BF16),
            vmem(2, 8, 8, 3072),
            pltpu.VMEM((256, 256), BF16),
            vmem(8, 8, 3072),
            vmem(CHUNKS, T, 4, 2, 8, 128),
            vmem(k, 2, T, 8, 128),
            vmem(k, 2, T, 2, 8, 128),
            vmem(k, T, 2, 8, 128),
            vmem(k, T, 4, 8, 128),
            vmem(k, T, 4, 8, 128),
            vmem(k, T, 8, 128),
            vmem(k, 2, T // 2, 8, 128),
            vmem(k, 2, T, 8, 128),
            vmem(CHUNKS, T * 8, 128),
            vmem(CHUNKS, 8, T, 128),
            vmem(2, 48, 128),
            vmem(48, 128),
            vmem(7, 48, 128),
            vmem(8, 48, 128),
            vmem(56, 128),
            vmem(56, 128),
            vmem(256, 128),
            vmem(7, 32, 128),
            vmem(4, 2, 2, 4, 16, 256),
            vmem(4, 2, 4, 16, 256),
            vmem(4, 2, 16, 256),
            vmem(4, 2, 2, 16, 256),
            vmem(4, 2, 16, 256),
            vmem(3, 2, 16, 256),
            vmem(2, 2, 8, 256),
            vmem(3, 8, 256),
            pltpu.SemaphoreType.DMA((CHUNKS + 3,)),
            pltpu.SemaphoreType.DMA((slots,)),
            pltpu.SemaphoreType.DMA((slots,)),
        ],
        compiler_params=pltpu.CompilerParams(collective_id=0, has_side_effects=True),
        name="sketch_and_exchange",
    )(ensemble, map_two, core_two, core_one, map_one, map_three, map_four)


def final_kernel(h_ref, three_ref, four_ref, i1_ref, i2_ref, i3_ref, i4_ref, out_ref, o1_ref, o2_ref, o3_ref, o4_ref, grown, lhs, block):
    step = pl.program_id(0)

    @pl.when(step == 0)
    def _():
        three = three_ref[...]
        three = jnp.concatenate([three, three], axis=0)
        for s in range(8):
            high, low = two_terms(h_ref[s])
            both = jnp.concatenate([high, low], axis=0)
            grown[pl.ds(s, 128, stride=8), :] = lax.dot_general(
                both, three, (((0,), (0,)), ((), ())), preferred_element_type=F32
            )
        for i in range(8):
            high, low = two_terms(grown[pl.ds(i * 128, 128), :].T)
            lhs[i * 128 : (i + 1) * 128, 0:128] = high
            lhs[i * 128 : (i + 1) * 128, 128:256] = low
        o1_ref[...] = i1_ref[...]
        o2_ref[...] = i2_ref[...]
        o3_ref[...] = i3_ref[...]
        o4_ref[...] = i4_ref[0:1]

    four = jnp.tile(four_ref[...].astype(F32), (16, 2))
    row = lax.broadcasted_iota(jnp.int32, (128, 256), 0) // 8
    col = lax.broadcasted_iota(jnp.int32, (128, 256), 1) // 128
    part = jnp.where(row == col + 2 * step, four, 0.0).astype(BF16)
    block[0:128] = part
    block[128:256] = part
    res = jnp.dot(lhs[...], block[...], preferred_element_type=F32)
    for e in range(2):
        out_ref[:, 0, e] = res[:, e * 128 : (e + 1) * 128].reshape(8, 128, 128)


def final(h, core_three, core_four, s1, s2, s3, s4):
    whole = lambda shape: pl.BlockSpec(shape, lambda i: (0,) * len(shape))
    return pl.pallas_call(
        final_kernel,
        grid=(8,),
        in_specs=[whole(a.shape) for a in (h, core_three, core_four, s1, s2, s3, s4)],
        out_specs=[
            pl.BlockSpec((8, 1, 2, 128, 128), lambda i: (0, i, 0, 0, 0)),
            whole((32, 64)),
            whole((8, 256)),
            whole((48, 256)),
            whole((1, 256)),
        ],
        out_shape=[
            jax.ShapeDtypeStruct((8, 8, 2, 128, 128), F32),
            jax.ShapeDtypeStruct((32, 64), F32),
            jax.ShapeDtypeStruct((8, 256), F32),
            jax.ShapeDtypeStruct((48, 256), F32),
            jax.ShapeDtypeStruct((1, 256), F32),
        ],
        scratch_shapes=[
            pltpu.VMEM((1024, 128), F32),
            pltpu.VMEM((1024, 256), BF16),
            pltpu.VMEM((256, 256), BF16),
        ],
        compiler_params=pltpu.CompilerParams(dimension_semantics=("arbitrary",)),
        name="final",
    )(h, core_three, core_four, s1, s2, s3, s4)


def on_device(
    ensemble, map_one, map_two, map_three, map_four, core_one, core_two, core_three, core_four
):
    h, s1, s2, s3, s4 = fused(ensemble, map_one, map_two, map_three, map_four, core_one, core_two)
    core, s1, s2, s3, s4 = final(h, core_three, core_four, s1, s2, s3, s4)
    return (s1.T, s2, s3, s4, core.reshape(128, 128, 128))


def solution(mesh):
    placed = (
        P(None, "sample", "space", None),
        P("space", None),
        P(),
        P(),
        P("sample", None),
        P(),
        P(),
        P(),
        P(),
    )
    return jax.shard_map(
        on_device,
        mesh=mesh,
        in_specs=placed,
        out_specs=(
            P("space", "sample"),
            P(("space", "sample"), None),
            P(),
            P("sample", None),
            P(None, ("space", "sample"), None),
        ),
        check_vma=False,
    )
```

```python
import jax
import jax.numpy as jnp
from jax import lax
from jax.experimental import pallas as pl
from jax.experimental.pallas import tpu as pltpu
from jax.sharding import PartitionSpec as P

F32 = jnp.float32
BF16 = jnp.bfloat16
MESH = pl.DeviceIdType.MESH
T = 8


def two_terms(value):
    high = value.astype(BF16)
    low = (value - high.astype(F32)).astype(BF16)
    return high, low


CHUNKS = 6
KINDS = "zzxzxx"
PLACE = (0, 1, 0, 2, 1, 2)


def fused_kernel(
    ens_ref, two_ref, ctwo_ref, cone_ref, one_hbm, three_hbm, four_hbm,
    h_ref, o1_hbm, o2_hbm, o3_hbm, o4_hbm,
    one_ref, three_ref, four_ref, o1_ref, o2_ref, o3_ref, o4_ref,
    xv, two, ctwo, cone, krao, cp, weight, cp_in, half, xa, xb, xr, za, zr, zs, zc, fin, parts,
    q_own, q_in, q_a, q_x, q_b, q_y, q_s, q_o, q_oi, s1_own, s1_in,
    s2, s2_in, s2_y, s2_r, s2_z,
    load_sem, send_sem, recv_sem,
):
    space = lax.axis_index("space")
    sample = lax.axis_index("sample")
    x, zl, c = space // 4, (space // 2) % 2, space % 2
    y, zh = sample // 2, sample % 2
    xs = [lax.rem(x + d, 4) for d in range(4)]
    ys = [lax.rem(y + d, 4) for d in range(4)]
    samples = [lax.rem(sample + d, 8) for d in range(8)]
    at = lambda px, pz: (px * 4 + pz * 2 + c, sample)
    mate = (x * 4 + zl * 2 + (1 - c), sample)
    zmate = at(x, 1 - zl)
    right, left = at(xs[1], zl), at(xs[3], zl)
    mates = [(space, samples[d]) for d in range(8)]

    barrier = pltpu.get_barrier_semaphore()
    spread = lambda d, e, f: (xs[d] * 4 + (1 - zl if e else zl) * 2 + c, y * 2 + (1 - zh if f else zh))
    around = [(d, e, f) for d in (2, 1, 3, 0) for e in (1, 0) for f in (1, 0) if (d, e, f) != (0, 0, 0)]
    peers = [mate] + [spread(*way) for way in around] + [(space, ys[d] * 2 + zh) for d in (1, 2, 3)]
    peers += [(space, ys[d] * 2 + 1 - zh) for d in (1, 2, 3)]
    for peer in peers:
        pl.semaphore_signal(barrier, inc=1, device_id=peer, device_id_type=MESH)

    def load(src, dst, slot):
        copy = pltpu.make_async_copy(src, dst, load_sem.at[slot])
        copy.start()
        return copy

    load_ctwo = load(ctwo_ref, ctwo, CHUNKS)
    loads = [load(ens_ref.at[pl.ds(0, T), 0], xv.at[pl.ds(0, T)], 0)]
    small = [
        load(one_hbm, one_ref, CHUNKS + 3),
        load(three_hbm, three_ref, CHUNKS + 4),
        load(four_hbm, four_ref, CHUNKS + 5),
    ]
    load_cone = load(cone_ref, cone, CHUNKS + 1)
    loads += [load(ens_ref.at[pl.ds(n * T, T), 0], xv.at[pl.ds(n * T, T)], n) for n in range(1, CHUNKS)]
    load_two = load(two_ref, two, CHUNKS + 2)
    weight[...] = jnp.zeros_like(weight)

    copies, stores = [], []

    def store(src, dst):
        stores.append(load(src, dst, CHUNKS + 6 + len(stores)))

    def send(src, dst, to):
        slot = len(copies)
        copy = pltpu.make_async_remote_copy(
            src_ref=src, dst_ref=dst, send_sem=send_sem.at[slot], recv_sem=recv_sem.at[slot],
            device_id=to, device_id_type=MESH,
        )
        copy.start()
        copies.append(copy)
        return copy

    def arrived(group):
        for copy in group:
            copy.wait_recv()

    far = xs[2]
    rows_in = T * 64
    core, st1, st2, st3, st4 = {}, {}, {}, {}, {}

    load_ctwo.wait()
    for copy in small:
        copy.wait()
    one = one_ref[...].astype(F32)
    four = four_ref[...].astype(F32)

    def project(n):
        loads[n].wait()
        block = xv[pl.ds(n * T, T)].reshape(rows_in, 1024)
        value = lax.dot_general(
            ctwo[...], block, (((0,), (1,)), ((), ())), preferred_element_type=F32
        ).reshape(8, 2, 8, rows_in)
        lanes = pl.ds(n * rows_in, rows_in)
        for e in range(2):
            cp[e, :, :, lanes] = value[:, e]
        if n == 0:
            pl.semaphore_wait(barrier, len(peers))
        core[n] = [send(cp.at[1 - c, :, :, lanes], cp_in.at[:, :, lanes], mate)]
        third = three_ref[n * T : (n + 1) * T, :].astype(F32)
        krao[n * rows_in : (n + 1) * rows_in, :] = (
            ((third * four)[:, None, :] * one[None]).astype(BF16).reshape(rows_in, 256)
        )

    def contract(n):
        arrived(core[n])
        rows = []
        for p in range(T // 2):
            lanes = pl.ds(n * rows_in + p * 128, 128)
            mine = cp[c, :, :, lanes].reshape(64, 128)
            theirs = cp_in[:, :, lanes].reshape(64, 128)
            rows.append(jnp.concatenate([mine, theirs], axis=1))
        high, low = two_terms(jnp.concatenate(rows, axis=0))
        res = jnp.dot(high, weight[...], preferred_element_type=F32)
        res = res + jnp.dot(low, weight[...], preferred_element_type=F32)
        for p in range(T // 2):
            for e in range(2):
                half[n, p * 2 + e] = res[p * 64 : (p + 1) * 64, e * 128 : (e + 1) * 128].reshape(4, 2, 8, 128)
        k = PLACE[n]
        if KINDS[n] == "x":
            st1[n] = [send(half.at[n, :, far, 0], xa.at[k, 0], right), send(half.at[n, :, far, 1], xa.at[k, 1], left)]
        else:
            st1[n] = [send(half.at[n, :, :, 1 - zl], za.at[k], zmate)]

    def stage_two(n):
        arrived(st1[n])
        k = PLACE[n]
        if KINDS[n] == "x":
            half[n, :, xs[1], 0] += xa[k, 0]
            half[n, :, xs[3], 1] += xa[k, 1]
            st2[n] = [send(half.at[n, :, xs[1]], xb.at[k, 0], right), send(half.at[n, :, xs[3]], xb.at[k, 1], left)]
        else:
            zr[k] = half[n, :, :, zl] + za[k]
            st3[n] = [send(zr.at[k, :, xs[d]], zc.at[k, d - 1], at(xs[d], zl)) for d in (2, 1, 3)]

    def stage_three(n):
        arrived(st2[n])
        k = PLACE[n]
        xr[k] = half[n, :, x] + xb[k, 0] + xb[k, 1]
        st3[n] = [send(xr.at[k, :, 1 - zl], zs.at[k], zmate)]

    def stage_four(n):
        arrived(st3[n])
        k = PLACE[n]
        if KINDS[n] == "x":
            value = xr[k, :, zl] + zs[k]
        else:
            value = zr[k, :, x] + zc[k, 0] + zc[k, 1] + zc[k, 2]
        fin[n] = value.reshape(T * 8, 128)
        for s in range(8):
            parts[n, s] = fin[n, pl.ds(s, T, stride=8), :]
        store(parts.at[n, sample], h_ref.at[sample, pl.ds(n * T, T)])
        st4[n] = [
            send(parts.at[n, samples[d]], h_ref.at[sample, pl.ds(n * T, T)], mates[d]) for d in range(7, 0, -1)
        ]

    def second_block(d):
        columns = pl.ds(pl.multiple_of(xs[d] * 256, 256), 256)
        s2[d] = lax.dot_general(
            xv[:, :, columns].reshape(48 * 64, 256), krao[...],
            (((0,), (0,)), ((), ())), preferred_element_type=F32,
        ).reshape(2, 2, 4, 16, 256)
        s2_core[d] = [send(s2.at[d, :, 1 - c], s2_in.at[d], mate)]

    def second_one(d):
        arrived(s2_core[d])
        s2_in[d] += s2[d, :, c]
        s2_one[d] = [
            send(s2_in.at[d, :, ys[e]], s2_y.at[d, e - 1], (space, ys[e] * 2 + zh)) for e in (2, 1, 3)
        ]

    def second_two(d):
        arrived(s2_one[d])
        total = s2_in[d, :, y] + s2_y[d, 0] + s2_y[d, 1] + s2_y[d, 2]
        s2_r[d] = total.reshape(2, 2, 8, 256)
        for way in around:
            if way[0] == d:
                _, e, f = way
                s2_two.append(send(
                    s2_r.at[d, 1 - zl if e else zl, 1 - zh if f else zh],
                    s2_z.at[d * 4 + e * 2 + f], spread(*way),
                ))

    def points(n, first):
        block = xv[pl.ds(n * T, T)].reshape(rows_in, 1024)
        third = three_ref[n * T : (n + 1) * T, :].astype(F32)
        proj = jnp.dot(block, two[...], preferred_element_type=F32).reshape(T, 64, 256)
        q = jnp.sum(proj * one[None], axis=1)
        q_own[0, pl.ds(n * T, T)] = q[:, :128]
        q_own[1, pl.ds(n * T, T)] = q[:, 128:]
        return first + jnp.sum(proj * third[:, None, :], axis=0)

    def q_one():
        return [send(q_own.at[1 - c], q_in, mate)]

    def q_two(group):
        arrived(group)
        total = q_in[...] + q_own[c]
        mine3 = jnp.where(c == 0, three_ref[:, :128], three_ref[:, 128:]).astype(F32)
        mine4 = jnp.where(c == 0, four[:, :128], four[:, 128:])
        q_a[pl.ds(0, 48)] = total * mine4
        q_a[pl.ds(48, 8)] = jnp.broadcast_to(jnp.sum(total * mine3, axis=0, keepdims=True), (8, 128))
        return [send(q_a, q_x.at[d - 1], at(xs[d], zl)) for d in (2, 1, 3)]

    def q_three(group):
        arrived(group)
        q_b[...] = q_a[...] + q_x[0] + q_x[1] + q_x[2]
        return [
            send(q_b.at[pl.ds(0, 48)], q_y.at[d - 1], (space, ys[d] * 2 + zh)) for d in (2, 1, 3)
        ]

    def q_four(group):
        arrived(group)
        q_s[0, pl.ds(0, 48)] = q_b[pl.ds(0, 48)] + q_y[0] + q_y[1] + q_y[2]
        q_s[0, pl.ds(48, 8)] = q_b[pl.ds(48, 8)]
        return [send(q_s.at[0], q_s.at[e * 2 + f], spread(0, e, f)) for e, f in ((0, 1), (1, 1), (1, 0))]

    def q_five(group):
        arrived(group)
        q_o[pl.ds(0, 48)] = (q_s[0] + q_s[1] + q_s[2] + q_s[3])[:48]
        q_o[pl.ds(48, 8)] = q_s[0, pl.ds(48, 8)] + q_s[2, pl.ds(48, 8)]
        return [send(q_o, q_oi, mate)]

    def one_sends():
        group = []
        for d in range(1, 8):
            rows = pl.ds(pl.multiple_of(samples[d] * 32, 32), 32)
            group.append(send(s1_own.at[rows], s1_in.at[d - 1], mates[d]))
        return group

    s2_core, s2_one, s2_two = {}, {}, []
    project(0)
    load_cone.wait()
    own = cone[pl.ds(pl.multiple_of(space * 64, 64), 64), :]
    other = cone[pl.ds(pl.multiple_of((x * 4 + zl * 2 + 1 - c) * 64, 64), 64), :]
    weight[0:64, 0:128] = own
    weight[64:128, 128:256] = own
    weight[128:192, 0:128] = other
    weight[192:256, 128:256] = other
    first = jnp.zeros((64, 256), F32)
    project(1)
    contract(0)
    project(2)
    project(3)
    contract(1)
    project(4)
    contract(2)
    project(5)
    contract(3)
    load_two.wait()
    first = points(0, first)
    contract(4)
    first = points(1, first)
    contract(5)
    for n in range(2, CHUNKS):
        first = points(n, first)
    q_wait = q_one()
    s1_own[...] = jnp.zeros_like(s1_own)
    s1_own[:, :64] = (first * four).T
    s1_wait = one_sends()

    stage_two(2)
    stage_two(0)
    second_block(2)
    q_wait = q_two(q_wait)
    stage_two(4)
    second_block(1)
    second_one(2)
    stage_two(5)
    stage_two(1)
    second_block(3)
    second_one(1)
    stage_three(2)
    second_block(0)
    second_one(3)
    q_wait = q_three(q_wait)
    second_two(2)
    second_one(0)
    stage_two(3)
    stage_four(0)
    second_two(1)
    stage_three(4)
    second_two(3)
    stage_three(5)
    stage_four(1)
    q_wait = q_four(q_wait)
    second_two(0)
    stage_four(2)
    stage_four(3)
    stage_four(4)
    q_wait = q_five(q_wait)
    stage_four(5)

    arrived(s1_wait)
    total = s1_own[pl.ds(pl.multiple_of(sample * 32, 32), 32)]
    for d in range(1, 8):
        total = total + s1_in[d - 1]
    o1_ref[...] = total[:, :64]
    store(o1_ref, o1_hbm)

    arrived(q_wait)
    here, there = q_o[...], q_oi[...]
    low = jnp.where(c == 0, here, there)
    top = jnp.where(c == 0, there, here)
    o3_ref[:, :128] = low[:48]
    o3_ref[:, 128:] = top[:48]
    o4_ref[:, :128] = low[48:49]
    o4_ref[:, 128:] = top[48:49]
    store(o3_ref, o3_hbm)
    store(o4_ref, o4_hbm)

    arrived(s2_two)
    total = s2_r[0, zl, zh]
    for d in range(1, 16):
        total = total + s2_z[d]
    o2_ref[...] = total
    store(o2_ref, o2_hbm)
    for n in range(CHUNKS):
        arrived(st4[n])
    for copy in stores:
        copy.wait()
    for copy in copies:
        copy.wait_send()


def fused(ensemble, map_one, map_two, map_three, map_four, core_one, core_two):
    k = CHUNKS // 2
    vmem = lambda *shape: pltpu.VMEM(shape, F32)
    there = pl.BlockSpec(memory_space=pl.ANY)
    slots = CHUNKS * 13 + 31 + 13 + 7
    return pl.pallas_call(
        fused_kernel,
        in_specs=[there] * 7,
        out_specs=[there] * 5,
        out_shape=[
            jax.ShapeDtypeStruct((8, 48, 128), F32),
            jax.ShapeDtypeStruct((32, 64), F32),
            jax.ShapeDtypeStruct((8, 256), F32),
            jax.ShapeDtypeStruct((48, 256), F32),
            jax.ShapeDtypeStruct((1, 256), F32),
        ],
        scratch_shapes=[
            pltpu.VMEM((64, 256), BF16),
            pltpu.VMEM((48, 256), BF16),
            pltpu.VMEM((1, 256), BF16),
            vmem(32, 64),
            vmem(8, 256),
            vmem(48, 256),
            vmem(1, 256),
            pltpu.VMEM((48, 64, 1024), BF16),
            pltpu.VMEM((1024, 256), BF16),
            pltpu.VMEM((1024, 128), BF16),
            pltpu.VMEM((1024, 128), BF16),
            pltpu.VMEM((48 * 64, 256), BF16),
            vmem(2, 8, 8, 3072),
            pltpu.VMEM((256, 256), BF16),
            vmem(8, 8, 3072),
            vmem(CHUNKS, T, 4, 2, 8, 128),
            vmem(k, 2, T, 8, 128),
            vmem(k, 2, T, 2, 8, 128),
            vmem(k, T, 2, 8, 128),
            vmem(k, T, 4, 8, 128),
            vmem(k, T, 4, 8, 128),
            vmem(k, T, 8, 128),
            vmem(k, 3, T, 8, 128),
            vmem(CHUNKS, T * 8, 128),
            vmem(CHUNKS, 8, T, 128),
            vmem(2, 48, 128),
            vmem(48, 128),
            vmem(56, 128),
            vmem(3, 56, 128),
            vmem(56, 128),
            vmem(3, 48, 128),
            vmem(4, 56, 128),
            vmem(56, 128),
            vmem(56, 128),
            vmem(256, 128),
            vmem(7, 32, 128),
            vmem(4, 2, 2, 4, 16, 256),
            vmem(4, 2, 4, 16, 256),
            vmem(4, 3, 2, 16, 256),
            vmem(4, 2, 2, 8, 256),
            vmem(16, 8, 256),
            pltpu.SemaphoreType.DMA((2 * CHUNKS + 10,)),
            pltpu.SemaphoreType.DMA((slots,)),
            pltpu.SemaphoreType.DMA((slots,)),
        ],
        compiler_params=pltpu.CompilerParams(collective_id=0, has_side_effects=True),
        name="sketch_and_exchange",
    )(ensemble, map_two, core_two, core_one, map_one, map_three, map_four)


def final_kernel(
    h_hbm, three_ref, four_ref, i1_ref, i2_ref, i3_ref, i4_ref,
    out_ref, o1_ref, o2_ref, o3_ref, o4_ref,
    h_ref, grown, lhs, blocks, result, sem,
):
    load = pltpu.make_async_copy(h_hbm, h_ref, sem.at[8])
    load.start()
    passed = [(i1_ref, o1_ref), (i2_ref, o2_ref), (i3_ref, o3_ref), (i4_ref, o4_ref)]
    passes = [pltpu.make_async_copy(src, dst, sem.at[9 + n]) for n, (src, dst) in enumerate(passed)]
    for copy in passes:
        copy.start()
    four = jnp.tile(four_ref[...].astype(F32), (16, 2))
    row = lax.broadcasted_iota(jnp.int32, (128, 256), 0) // 8
    col = lax.broadcasted_iota(jnp.int32, (128, 256), 1) // 128
    for j in range(8):
        part = jnp.where(row == col + 2 * j, four, 0.0).astype(BF16)
        blocks[j, 0:128] = part
        blocks[j, 128:256] = part
    three = three_ref[...]
    three = jnp.concatenate([three, three], axis=0)
    load.wait()
    for s in range(8):
        high, low = two_terms(h_ref[s])
        both = jnp.concatenate([high, low], axis=0)
        grown[pl.ds(s, 128, stride=8), :] = lax.dot_general(
            both, three, (((0,), (0,)), ((), ())), preferred_element_type=F32
        )
    for i in range(8):
        high, low = two_terms(grown[pl.ds(i * 128, 128), :].T)
        lhs[i * 128 : (i + 1) * 128, 0:128] = high
        lhs[i * 128 : (i + 1) * 128, 128:256] = low
    writes = []
    for j in range(8):
        res = jnp.dot(lhs[...], blocks[j], preferred_element_type=F32)
        for e in range(2):
            result[j, :, e] = res[:, e * 128 : (e + 1) * 128].reshape(8, 128, 128)
        copy = pltpu.make_async_copy(result.at[j], out_ref.at[:, j], sem.at[j])
        copy.start()
        writes.append(copy)
    for copy in writes + passes:
        copy.wait()


def final(h, core_three, core_four, s1, s2, s3, s4):
    here = pl.BlockSpec(memory_space=pltpu.VMEM)
    there = pl.BlockSpec(memory_space=pl.ANY)
    return pl.pallas_call(
        final_kernel,
        in_specs=[there, here, here] + [there] * 4,
        out_specs=[there] * 5,
        out_shape=[
            jax.ShapeDtypeStruct((8, 8, 2, 128, 128), F32),
            jax.ShapeDtypeStruct((32, 64), F32),
            jax.ShapeDtypeStruct((8, 256), F32),
            jax.ShapeDtypeStruct((48, 256), F32),
            jax.ShapeDtypeStruct((1, 256), F32),
        ],
        scratch_shapes=[
            pltpu.VMEM((8, 48, 128), F32),
            pltpu.VMEM((1024, 128), F32),
            pltpu.VMEM((1024, 256), BF16),
            pltpu.VMEM((8, 256, 256), BF16),
            pltpu.VMEM((8, 8, 2, 128, 128), F32),
            pltpu.SemaphoreType.DMA((13,)),
        ],
        name="final",
    )(h, core_three, core_four, s1, s2, s3, s4)


def on_device(
    ensemble, map_one, map_two, map_three, map_four, core_one, core_two, core_three, core_four
):
    h, s1, s2, s3, s4 = fused(ensemble, map_one, map_two, map_three, map_four, core_one, core_two)
    core, s1, s2, s3, s4 = final(h, core_three, core_four, s1, s2, s3, s4)
    return (s1.T, s2, s3, s4, core.reshape(128, 128, 128))


def solution(mesh):
    placed = (
        P(None, "sample", "space", None),
        P("space", None),
        P(),
        P(),
        P("sample", None),
        P(),
        P(),
        P(),
        P(),
    )
    return jax.shard_map(
        on_device,
        mesh=mesh,
        in_specs=placed,
        out_specs=(
            P("space", "sample"),
            P(("space", "sample"), None),
            P(),
            P("sample", None),
            P(None, ("space", "sample"), None),
        ),
        check_vma=False,
    )
```

```python
import jax
import jax.numpy as jnp
from jax import lax
from jax.experimental import pallas as pl
from jax.experimental.pallas import tpu as pltpu
from jax.sharding import PartitionSpec as P

F32 = jnp.float32
BF16 = jnp.bfloat16
MESH = pl.DeviceIdType.MESH
T = 8


def two_terms(value):
    high = value.astype(BF16)
    low = (value - high.astype(F32)).astype(BF16)
    return high, low


CHUNKS = 6
KINDS = "zxxzxz"
PLACE = (0, 0, 1, 1, 2, 2)


def fused_kernel(
    ens_ref, two_ref, ctwo_ref, cone_ref, one_hbm, three_hbm, four_hbm,
    h_ref, o1_hbm, o2_hbm, o3_hbm, o4_hbm,
    one_ref, three_ref, four_ref, o1_ref, o2_ref, o3_ref, o4_ref,
    xv, two, ctwo, turned, cone, krao, cp, weight, cp_in, half, xa, xb, xr, za, zr, zs, zc, fin, parts,
    q_own, q_in, q_a, q_x, q_b, q_y, q_s, s1_own, s1_in,
    s2, s2_in, s2_y, s2_r, s2_z,
    load_sem, send_sem, recv_sem,
):
    space = lax.axis_index("space")
    sample = lax.axis_index("sample")
    x, zl, c = space // 4, (space // 2) % 2, space % 2
    y, zh = sample // 2, sample % 2
    xs = [lax.rem(x + d, 4) for d in range(4)]
    ys = [lax.rem(y + d, 4) for d in range(4)]
    samples = [lax.rem(sample + d, 8) for d in range(8)]
    at = lambda px, pz: (px * 4 + pz * 2 + c, sample)
    mate = (x * 4 + zl * 2 + (1 - c), sample)
    zmate = at(x, 1 - zl)
    right, left = at(xs[1], zl), at(xs[3], zl)
    mates = [(space, samples[d]) for d in range(8)]

    barrier = pltpu.get_barrier_semaphore()
    spread = lambda d, e, f: (xs[d] * 4 + (1 - zl if e else zl) * 2 + c, y * 2 + (1 - zh if f else zh))
    around = [(d, e, f) for d in (2, 1, 3, 0) for e in (1, 0) for f in (1, 0) if (d, e, f) != (0, 0, 0)]
    peers = [mate] + [spread(*way) for way in around] + [(space, ys[d] * 2 + zh) for d in (1, 2, 3)]
    peers += [(space, ys[d] * 2 + 1 - zh) for d in (1, 2, 3)]
    peers += [(spread(0, e, f)[0] + 1 - 2 * c, spread(0, e, f)[1]) for e, f in ((0, 1), (1, 0), (1, 1))]
    for peer in peers:
        pl.semaphore_signal(barrier, inc=1, device_id=peer, device_id_type=MESH)

    def load(src, dst, slot):
        copy = pltpu.make_async_copy(src, dst, load_sem.at[slot])
        copy.start()
        return copy

    load_ctwo = load(ctwo_ref, ctwo, CHUNKS)
    loads = [load(ens_ref.at[pl.ds(0, T), 0], xv.at[pl.ds(0, T)], 0)]
    small = [
        load(one_hbm, one_ref, CHUNKS + 3),
        load(three_hbm, three_ref, CHUNKS + 4),
        load(four_hbm, four_ref, CHUNKS + 5),
    ]
    load_cone = load(cone_ref, cone, CHUNKS + 1)
    loads += [load(ens_ref.at[pl.ds(n * T, T), 0], xv.at[pl.ds(n * T, T)], n) for n in range(1, CHUNKS)]
    load_two = load(two_ref, two, CHUNKS + 2)
    weight[...] = jnp.zeros_like(weight)

    chunk_lanes = lambda n: pl.ds(n * T * 64, T * 64)
    k = CHUNKS // 2
    kinds = {
        "core": (CHUNKS, lambda n: cp_in.at[:, :, chunk_lanes(n)], cp_in),
        "xa": (k, lambda n: xa.at[n], xa),
        "xb": (k, lambda n: xb.at[n], xb),
        "za": (k, lambda n: za.at[n], za),
        "zs": (k, lambda n: zs.at[n], zs),
        "zc": (k, lambda n: zc.at[n], zc),
        "h": (1, None, h_ref.at[pl.ds(0, 7)]),
        "sc": (4, lambda n: s2_in.at[n], s2_in),
        "sy": (4, lambda n: s2_y.at[n], s2_y),
        "sz": (1, None, s2_z.at[pl.ds(1, 15)]),
        "qc": (1, None, q_in),
        "qx": (1, None, q_x),
        "qy": (1, None, q_y),
        "qz": (1, None, q_s.at[pl.ds(1, 7)]),
        "one": (1, None, s1_in),
    }
    base, total_slots = {}, 0
    for kind, (count, _, _) in kinds.items():
        base[kind] = total_slots
        total_slots += count
    order = list(kinds)

    def send(kind, n, src, dst, to):
        pltpu.make_async_remote_copy(
            src_ref=src, dst_ref=dst, send_sem=send_sem.at[order.index(kind)], recv_sem=recv_sem.at[base[kind] + n],
            device_id=to, device_id_type=MESH,
        ).start()

    def arrived(kind, n=0):
        count, part, whole = kinds[kind]
        ref = whole if part is None else part(n)
        pltpu.make_async_copy(ref, ref, recv_sem.at[base[kind] + n]).wait()

    def sent(kind):
        ref = kinds[kind][2]
        pltpu.make_async_copy(ref, ref, send_sem.at[order.index(kind)]).wait()

    stores = []

    def store(src, dst):
        stores.append(load(src, dst, CHUNKS + 7 + len(stores)))

    far = xs[2]
    rows_in = T * 64

    load_ctwo.wait()
    turned[...] = ctwo[...].T
    for copy in small:
        copy.wait()
    one = one_ref[...].astype(F32)
    four = four_ref[...].astype(F32)

    def project(n):
        loads[n].wait()
        block = xv[pl.ds(n * T, T)].reshape(rows_in, 1024)
        value = lax.dot_general(
            turned[...], block, (((1,), (1,)), ((), ())), preferred_element_type=F32
        ).reshape(8, 2, 8, rows_in)
        lanes = pl.ds(n * rows_in, rows_in)
        for e in range(2):
            cp[e, :, :, lanes] = value[:, e]
        if n == 0:
            pl.semaphore_wait(barrier, len(peers))
        send("core", n, cp.at[1 - c, :, :, lanes], cp_in.at[:, :, lanes], mate)
        third = three_ref[n * T : (n + 1) * T, :].astype(F32)
        krao[n * rows_in : (n + 1) * rows_in, :] = (
            ((third * four)[:, None, :] * one[None]).astype(BF16).reshape(rows_in, 256)
        )

    def contract(n):
        arrived("core", n)
        rows = []
        for p in range(T // 2):
            lanes = pl.ds(n * rows_in + p * 128, 128)
            mine = cp[c, :, :, lanes].reshape(64, 128)
            theirs = cp_in[:, :, lanes].reshape(64, 128)
            rows.append(jnp.concatenate([mine, theirs], axis=1))
        high, low = two_terms(jnp.concatenate(rows, axis=0))
        res = jnp.dot(high, weight[...], preferred_element_type=F32)
        res = res + jnp.dot(low, weight[...], preferred_element_type=F32)
        for p in range(T // 2):
            for e in range(2):
                half[n, p * 2 + e] = res[p * 64 : (p + 1) * 64, e * 128 : (e + 1) * 128].reshape(4, 2, 8, 128)
        k = PLACE[n]
        if KINDS[n] == "x":
            send("xa", k, half.at[n, :, far, 0], xa.at[k, 0], right)
            send("xa", k, half.at[n, :, far, 1], xa.at[k, 1], left)
        else:
            send("za", k, half.at[n, :, :, 1 - zl], za.at[k], zmate)

    def stage_two(n):
        k = PLACE[n]
        arrived("xa" if KINDS[n] == "x" else "za", k)
        if KINDS[n] == "x":
            half[n, :, xs[1], 0] += xa[k, 0]
            half[n, :, xs[3], 1] += xa[k, 1]
            send("xb", k, half.at[n, :, xs[1]], xb.at[k, 0], right)
            send("xb", k, half.at[n, :, xs[3]], xb.at[k, 1], left)
        else:
            zr[k] = half[n, :, :, zl] + za[k]
            for d in (2, 1, 3):
                send("zc", k, zr.at[k, :, xs[d]], zc.at[k, d - 1], at(xs[d], zl))

    def stage_three(n):
        k = PLACE[n]
        arrived("xb", k)
        xr[k] = half[n, :, x] + xb[k, 0] + xb[k, 1]
        send("zs", k, xr.at[k, :, 1 - zl], zs.at[k], zmate)

    def stage_four(n):
        k = PLACE[n]
        arrived("zs" if KINDS[n] == "x" else "zc", k)
        if KINDS[n] == "x":
            value = xr[k, :, zl] + zs[k]
        else:
            value = zr[k, :, x] + zc[k, 0] + zc[k, 1] + zc[k, 2]
        fin[n] = value.reshape(T * 8, 128)
        for s in range(8):
            parts[n, s] = fin[n, pl.ds(s, T, stride=8), :]
        pltpu.make_async_copy(parts.at[n, sample], h_ref.at[sample, pl.ds(n * T, T)], load_sem.at[CHUNKS + 6]).start()
        for d in (5, 4, 3, 6, 2, 7, 1):
            send("h", 0, parts.at[n, samples[d]], h_ref.at[sample, pl.ds(n * T, T)], mates[d])

    def second_block(d):
        columns = pl.ds(pl.multiple_of(xs[d] * 256, 256), 256)
        s2[d] = lax.dot_general(
            xv[:, :, columns].reshape(48 * 64, 256), krao[...],
            (((0,), (0,)), ((), ())), preferred_element_type=F32,
        ).reshape(2, 2, 4, 16, 256)
        send("sc", d, s2.at[d, :, 1 - c], s2_in.at[d], mate)

    def second_one(d):
        arrived("sc", d)
        s2_in[d] += s2[d, :, c]
        for e in (2, 1, 3):
            send("sy", d, s2_in.at[d, :, ys[e]], s2_y.at[d, e - 1], (space, ys[e] * 2 + zh))

    def second_two(d):
        arrived("sy", d)
        total = s2_in[d, :, y] + s2_y[d, 0] + s2_y[d, 1] + s2_y[d, 2]
        s2_r[d] = total.reshape(2, 2, 8, 256)
        for way in around:
            if way[0] == d:
                _, e, f = way
                send(
                    "sz", 0, s2_r.at[d, 1 - zl if e else zl, 1 - zh if f else zh],
                    s2_z.at[d * 4 + e * 2 + f], spread(*way),
                )

    def points(n, first):
        block = xv[pl.ds(n * T, T)].reshape(rows_in, 1024)
        third = three_ref[n * T : (n + 1) * T, :].astype(F32)
        proj = jnp.dot(block, two[...], preferred_element_type=F32).reshape(T, 64, 256)
        q = jnp.sum(proj * one[None], axis=1)
        q_own[0, pl.ds(n * T, T)] = q[:, :128]
        q_own[1, pl.ds(n * T, T)] = q[:, 128:]
        return first + jnp.sum(proj * third[:, None, :], axis=0)

    def q_one():
        send("qc", 0, q_own.at[1 - c], q_in, mate)

    def q_two():
        arrived("qc")
        total = q_in[...] + q_own[c]
        mine3 = jnp.where(c == 0, three_ref[:, :128], three_ref[:, 128:]).astype(F32)
        mine4 = jnp.where(c == 0, four[:, :128], four[:, 128:])
        q_a[pl.ds(0, 48)] = total * mine4
        q_a[pl.ds(48, 8)] = jnp.broadcast_to(jnp.sum(total * mine3, axis=0, keepdims=True), (8, 128))
        for d in (2, 1, 3):
            send("qx", 0, q_a, q_x.at[d - 1], at(xs[d], zl))

    def q_three():
        arrived("qx")
        q_b[...] = q_a[...] + q_x[0] + q_x[1] + q_x[2]
        for d in (2, 1, 3):
            send("qy", 0, q_b.at[pl.ds(0, 48)], q_y.at[d - 1], (space, ys[d] * 2 + zh))

    def q_four():
        arrived("qy")
        q_s[0, pl.ds(0, 48)] = q_b[pl.ds(0, 48)] + q_y[0] + q_y[1] + q_y[2]
        q_s[0, pl.ds(48, 8)] = q_b[pl.ds(48, 8)]
        for e, f in ((0, 1), (1, 1), (1, 0), (0, 0)):
            slot = e * 2 + f
            px, py = spread(0, e, f)
            send("qz", 0, q_s.at[0], q_s.at[4 + slot], (px + 1 - 2 * c, py))
            if slot:
                send("qz", 0, q_s.at[0], q_s.at[slot], (px, py))

    def one_sends():
        for d in range(1, 8):
            rows = pl.ds(pl.multiple_of(samples[d] * 32, 32), 32)
            send("one", 0, s1_own.at[rows], s1_in.at[d - 1], mates[d])

    project(0)
    load_cone.wait()
    own = cone[pl.ds(pl.multiple_of(space * 64, 64), 64), :]
    other = cone[pl.ds(pl.multiple_of((x * 4 + zl * 2 + 1 - c) * 64, 64), 64), :]
    weight[0:64, 0:128] = own
    weight[64:128, 128:256] = own
    weight[128:192, 0:128] = other
    weight[192:256, 128:256] = other
    first = jnp.zeros((64, 256), F32)
    project(1)
    project(2)
    contract(0)
    project(3)
    contract(1)
    project(4)
    contract(2)
    project(5)
    contract(3)
    contract(4)
    load_two.wait()
    for n in range(0, 3):
        first = points(n, first)
    stage_two(1)
    contract(5)
    stage_two(0)
    for n in range(3, CHUNKS):
        first = points(n, first)
    q_one()
    stage_two(2)
    stage_two(4)
    second_block(2)
    q_two()
    second_block(1)
    second_one(2)
    stage_three(1)
    stage_two(3)
    second_block(3)
    second_one(1)
    stage_three(2)
    second_block(0)
    stage_two(5)
    q_three()
    s1_own[...] = jnp.zeros_like(s1_own)
    s1_own[:, :64] = (first * four).T
    second_one(3)
    stage_four(1)
    second_one(0)
    one_sends()
    stage_three(4)
    second_two(2)
    second_two(1)
    q_four()
    stage_four(0)
    stage_four(2)
    second_two(3)
    stage_four(4)
    stage_four(3)
    second_two(0)
    stage_four(5)

    arrived("one")
    total = s1_own[pl.ds(pl.multiple_of(sample * 32, 32), 32)]
    for d in range(1, 8):
        total = total + s1_in[d - 1]
    o1_ref[...] = total[:, :64]
    store(o1_ref, o1_hbm)

    arrived("qz")
    here = q_s[0, pl.ds(0, 48)] + q_s[1, pl.ds(0, 48)] + q_s[2, pl.ds(0, 48)] + q_s[3, pl.ds(0, 48)]
    there = q_s[4, pl.ds(0, 48)] + q_s[5, pl.ds(0, 48)] + q_s[6, pl.ds(0, 48)] + q_s[7, pl.ds(0, 48)]
    low = jnp.where(c == 0, here, there)
    top = jnp.where(c == 0, there, here)
    o3_ref[:, :128] = low
    o3_ref[:, 128:] = top
    here = q_s[0, pl.ds(48, 1)] + q_s[2, pl.ds(48, 1)]
    there = q_s[4, pl.ds(48, 1)] + q_s[6, pl.ds(48, 1)]
    o4_ref[:, :128] = jnp.where(c == 0, here, there)
    o4_ref[:, 128:] = jnp.where(c == 0, there, here)
    store(o3_ref, o3_hbm)
    store(o4_ref, o4_hbm)

    arrived("sz")
    total = s2_r[0, zl, zh]
    for d in range(1, 16):
        total = total + s2_z[d]
    o2_ref[...] = total
    store(o2_ref, o2_hbm)
    arrived("h")
    for copy in stores:
        copy.wait()
    pltpu.make_async_copy(h_ref.at[0], h_ref.at[0], load_sem.at[CHUNKS + 6]).wait()
    for kind in order:
        sent(kind)


def fused(ensemble, map_one, map_two, map_three, map_four, core_one, core_two):
    k = CHUNKS // 2
    vmem = lambda *shape: pltpu.VMEM(shape, F32)
    there = pl.BlockSpec(memory_space=pl.ANY)
    return pl.pallas_call(
        fused_kernel,
        in_specs=[there] * 7,
        out_specs=[there] * 5,
        out_shape=[
            jax.ShapeDtypeStruct((8, 48, 128), F32),
            jax.ShapeDtypeStruct((32, 64), F32),
            jax.ShapeDtypeStruct((8, 256), F32),
            jax.ShapeDtypeStruct((48, 256), F32),
            jax.ShapeDtypeStruct((1, 256), F32),
        ],
        scratch_shapes=[
            pltpu.VMEM((64, 256), BF16),
            pltpu.VMEM((48, 256), BF16),
            pltpu.VMEM((1, 256), BF16),
            vmem(32, 64),
            vmem(8, 256),
            vmem(48, 256),
            vmem(1, 256),
            pltpu.VMEM((48, 64, 1024), BF16),
            pltpu.VMEM((1024, 256), BF16),
            pltpu.VMEM((1024, 128), BF16),
            pltpu.VMEM((128, 1024), BF16),
            pltpu.VMEM((1024, 128), BF16),
            pltpu.VMEM((48 * 64, 256), BF16),
            vmem(2, 8, 8, 3072),
            pltpu.VMEM((256, 256), BF16),
            vmem(8, 8, 3072),
            vmem(CHUNKS, T, 4, 2, 8, 128),
            vmem(k, 2, T, 8, 128),
            vmem(k, 2, T, 2, 8, 128),
            vmem(k, T, 2, 8, 128),
            vmem(k, T, 4, 8, 128),
            vmem(k, T, 4, 8, 128),
            vmem(k, T, 8, 128),
            vmem(k, 3, T, 8, 128),
            vmem(CHUNKS, T * 8, 128),
            vmem(CHUNKS, 8, T, 128),
            vmem(2, 48, 128),
            vmem(48, 128),
            vmem(56, 128),
            vmem(3, 56, 128),
            vmem(56, 128),
            vmem(3, 48, 128),
            vmem(8, 56, 128),
            vmem(256, 128),
            vmem(7, 32, 128),
            vmem(4, 2, 2, 4, 16, 256),
            vmem(4, 2, 4, 16, 256),
            vmem(4, 3, 2, 16, 256),
            vmem(4, 2, 2, 8, 256),
            vmem(16, 8, 256),
            pltpu.SemaphoreType.DMA((CHUNKS + 11,)),
            pltpu.SemaphoreType.DMA((15,)),
            pltpu.SemaphoreType.DMA((36,)),
        ],
        compiler_params=pltpu.CompilerParams(collective_id=0, has_side_effects=True),
        name="sketch_and_exchange",
    )(ensemble, map_two, core_two, core_one, map_one, map_three, map_four)


def final_kernel(
    h_hbm, three_ref, four_ref, i1_ref, i2_ref, i3_ref, i4_ref,
    out_ref, o1_ref, o2_ref, o3_ref, o4_ref,
    h_ref, grown, lhs, blocks, result, sem,
):
    load = pltpu.make_async_copy(h_hbm, h_ref, sem.at[8])
    load.start()
    passed = [(i1_ref, o1_ref), (i2_ref, o2_ref), (i3_ref, o3_ref), (i4_ref, o4_ref)]
    passes = [pltpu.make_async_copy(src, dst, sem.at[9 + n]) for n, (src, dst) in enumerate(passed)]
    for copy in passes:
        copy.start()
    four = jnp.tile(four_ref[...].astype(F32), (16, 2))
    row = lax.broadcasted_iota(jnp.int32, (128, 256), 0) // 8
    col = lax.broadcasted_iota(jnp.int32, (128, 256), 1) // 128
    for j in range(8):
        part = jnp.where(row == col + 2 * j, four, 0.0).astype(BF16)
        blocks[j, 0:128] = part
        blocks[j, 128:256] = part
    three = three_ref[...]
    three = jnp.concatenate([three, three], axis=0)
    load.wait()
    for s in range(8):
        high, low = two_terms(h_ref[s])
        both = jnp.concatenate([high, low], axis=0)
        grown[pl.ds(s, 128, stride=8), :] = lax.dot_general(
            both, three, (((0,), (0,)), ((), ())), preferred_element_type=F32
        )
    for i in range(8):
        high, low = two_terms(grown[pl.ds(i * 128, 128), :].T)
        lhs[i * 128 : (i + 1) * 128, 0:128] = high
        lhs[i * 128 : (i + 1) * 128, 128:256] = low
    writes = []
    for j in range(8):
        res = jnp.dot(lhs[...], blocks[j], preferred_element_type=F32)
        for e in range(2):
            result[j, :, e] = res[:, e * 128 : (e + 1) * 128].reshape(8, 128, 128)
        copy = pltpu.make_async_copy(result.at[j], out_ref.at[:, j], sem.at[j])
        copy.start()
        writes.append(copy)
    for copy in writes + passes:
        copy.wait()


def final(h, core_three, core_four, s1, s2, s3, s4):
    here = pl.BlockSpec(memory_space=pltpu.VMEM)
    there = pl.BlockSpec(memory_space=pl.ANY)
    return pl.pallas_call(
        final_kernel,
        in_specs=[there, here, here] + [there] * 4,
        out_specs=[there] * 5,
        out_shape=[
            jax.ShapeDtypeStruct((8, 8, 2, 128, 128), F32),
            jax.ShapeDtypeStruct((32, 64), F32),
            jax.ShapeDtypeStruct((8, 256), F32),
            jax.ShapeDtypeStruct((48, 256), F32),
            jax.ShapeDtypeStruct((1, 256), F32),
        ],
        scratch_shapes=[
            pltpu.VMEM((8, 48, 128), F32),
            pltpu.VMEM((1024, 128), F32),
            pltpu.VMEM((1024, 256), BF16),
            pltpu.VMEM((8, 256, 256), BF16),
            pltpu.VMEM((8, 8, 2, 128, 128), F32),
            pltpu.SemaphoreType.DMA((13,)),
        ],
        name="final",
    )(h, core_three, core_four, s1, s2, s3, s4)


def on_device(
    ensemble, map_one, map_two, map_three, map_four, core_one, core_two, core_three, core_four
):
    h, s1, s2, s3, s4 = fused(ensemble, map_one, map_two, map_three, map_four, core_one, core_two)
    core, s1, s2, s3, s4 = final(h, core_three, core_four, s1, s2, s3, s4)
    return (s1.T, s2, s3, s4, core.reshape(128, 128, 128))


def solution(mesh):
    placed = (
        P(None, "sample", "space", None),
        P("space", None),
        P(),
        P(),
        P("sample", None),
        P(),
        P(),
        P(),
        P(),
    )
    return jax.shard_map(
        on_device,
        mesh=mesh,
        in_specs=placed,
        out_specs=(
            P("space", "sample"),
            P(("space", "sample"), None),
            P(),
            P("sample", None),
            P(None, ("space", "sample"), None),
        ),
        check_vma=False,
    )
```

```python
import jax
import jax.numpy as jnp
from jax import lax
from jax.experimental import pallas as pl
from jax.experimental.pallas import tpu as pltpu
from jax.sharding import PartitionSpec as P

F32 = jnp.float32
BF16 = jnp.bfloat16
MESH = pl.DeviceIdType.MESH
T = 8


def two_terms(value):
    high = value.astype(BF16)
    low = (value - high.astype(F32)).astype(BF16)
    return high, low


CHUNKS = 6
KINDS = "zxxzxz"
PLACE = (0, 0, 1, 1, 2, 2)


def fused_kernel(
    ens_ref, two_ref, ctwo_ref, cone_ref, one_hbm, three_hbm, four_hbm, cthree_hbm, cfour_hbm,
    h_ref, o1_ref, o2_ref, o3_ref, o4_ref, cthree_ref, cfour_ref,
    one_ref, three_ref, four_ref,
    xv, two, ctwo, turned, cone, krao, cp, weight, cp_in, half, xa, xb, xr, za, zr, zs, zc, fin, parts,
    q_own, q_in, q_a, q_x, q_b, q_y, q_s, s1_own, s1_in,
    s2, s2_in, s2_y, s2_r, s2_z,
    load_sem, send_sem, recv_sem,
):
    space = lax.axis_index("space")
    sample = lax.axis_index("sample")
    x, zl, c = space // 4, (space // 2) % 2, space % 2
    y, zh = sample // 2, sample % 2
    xs = [lax.rem(x + d, 4) for d in range(4)]
    ys = [lax.rem(y + d, 4) for d in range(4)]
    samples = [lax.rem(sample + d, 8) for d in range(8)]
    at = lambda px, pz: (px * 4 + pz * 2 + c, sample)
    mate = (x * 4 + zl * 2 + (1 - c), sample)
    zmate = at(x, 1 - zl)
    right, left = at(xs[1], zl), at(xs[3], zl)
    mates = [(space, samples[d]) for d in range(8)]

    barrier = pltpu.get_barrier_semaphore()
    spread = lambda d, e, f: (xs[d] * 4 + (1 - zl if e else zl) * 2 + c, y * 2 + (1 - zh if f else zh))
    around = [(d, e, f) for d in (2, 1, 3, 0) for e in (1, 0) for f in (1, 0) if (d, e, f) != (0, 0, 0)]
    peers = [mate] + [spread(*way) for way in around] + [(space, ys[d] * 2 + zh) for d in (1, 2, 3)]
    peers += [(space, ys[d] * 2 + 1 - zh) for d in (1, 2, 3)]
    peers += [(spread(0, e, f)[0] + 1 - 2 * c, spread(0, e, f)[1]) for e, f in ((0, 1), (1, 0), (1, 1))]
    for peer in peers:
        pl.semaphore_signal(barrier, inc=1, device_id=peer, device_id_type=MESH)

    def load(src, dst, slot):
        copy = pltpu.make_async_copy(src, dst, load_sem.at[slot])
        copy.start()
        return copy

    load_ctwo = load(ctwo_ref, ctwo, CHUNKS)
    loads = [load(ens_ref.at[pl.ds(0, T), 0], xv.at[pl.ds(0, T)], 0)]
    small = [
        load(one_hbm, one_ref, CHUNKS + 3),
        load(three_hbm, three_ref, CHUNKS + 4),
        load(four_hbm, four_ref, CHUNKS + 5),
    ]
    load_cone = load(cone_ref, cone, CHUNKS + 1)
    loads += [load(ens_ref.at[pl.ds(n * T, T), 0], xv.at[pl.ds(n * T, T)], n) for n in range(1, CHUNKS)]
    load_two = load(two_ref, two, CHUNKS + 2)
    late = [load(cthree_hbm, cthree_ref, CHUNKS + 6), load(cfour_hbm, cfour_ref, CHUNKS + 7)]
    weight[...] = jnp.zeros_like(weight)

    chunk_lanes = lambda n: pl.ds(n * T * 64, T * 64)
    k = CHUNKS // 2
    kinds = {
        "core": (CHUNKS, lambda n: cp_in.at[:, :, chunk_lanes(n)], cp_in),
        "xa": (k, lambda n: xa.at[n], xa),
        "xb": (k, lambda n: xb.at[n], xb),
        "za": (k, lambda n: za.at[n], za),
        "zs": (k, lambda n: zs.at[n], zs),
        "zc": (k, lambda n: zc.at[n], zc),
        "h": (1, None, h_ref.at[pl.ds(0, 7)]),
        "sc": (4, lambda n: s2_in.at[n], s2_in),
        "sy": (4, lambda n: s2_y.at[n], s2_y),
        "sz": (1, None, s2_z.at[pl.ds(1, 15)]),
        "qc": (1, None, q_in),
        "qx": (1, None, q_x),
        "qy": (1, None, q_y),
        "qz": (1, None, q_s.at[pl.ds(1, 7)]),
        "one": (1, None, s1_in),
    }
    base, total_slots = {}, 0
    for kind, (count, _, _) in kinds.items():
        base[kind] = total_slots
        total_slots += count
    order = list(kinds)

    def send(kind, n, src, dst, to):
        pltpu.make_async_remote_copy(
            src_ref=src, dst_ref=dst, send_sem=send_sem.at[order.index(kind)], recv_sem=recv_sem.at[base[kind] + n],
            device_id=to, device_id_type=MESH,
        ).start()

    def arrived(kind, n=0):
        count, part, whole = kinds[kind]
        ref = whole if part is None else part(n)
        pltpu.make_async_copy(ref, ref, recv_sem.at[base[kind] + n]).wait()

    def sent(kind):
        ref = kinds[kind][2]
        pltpu.make_async_copy(ref, ref, send_sem.at[order.index(kind)]).wait()

    far = xs[2]
    rows_in = T * 64

    load_ctwo.wait()
    turned[...] = ctwo[...].T
    for copy in small:
        copy.wait()
    one = one_ref[...].astype(F32)
    four = four_ref[...].astype(F32)

    def project(n):
        loads[n].wait()
        block = xv[pl.ds(n * T, T)].reshape(rows_in, 1024)
        value = lax.dot_general(
            turned[...], block, (((1,), (1,)), ((), ())), preferred_element_type=F32
        ).reshape(8, 2, 8, rows_in)
        lanes = pl.ds(n * rows_in, rows_in)
        for e in range(2):
            cp[e, :, :, lanes] = value[:, e]
        if n == 0:
            pl.semaphore_wait(barrier, len(peers))
        send("core", n, cp.at[1 - c, :, :, lanes], cp_in.at[:, :, lanes], mate)
        third = three_ref[n * T : (n + 1) * T, :].astype(F32)
        krao[n * rows_in : (n + 1) * rows_in, :] = (
            ((third * four)[:, None, :] * one[None]).astype(BF16).reshape(rows_in, 256)
        )

    def contract(n):
        arrived("core", n)
        rows = []
        for p in range(T // 2):
            lanes = pl.ds(n * rows_in + p * 128, 128)
            mine = cp[c, :, :, lanes].reshape(64, 128)
            theirs = cp_in[:, :, lanes].reshape(64, 128)
            rows.append(jnp.concatenate([mine, theirs], axis=1))
        high, low = two_terms(jnp.concatenate(rows, axis=0))
        res = jnp.dot(high, weight[...], preferred_element_type=F32)
        res = res + jnp.dot(low, weight[...], preferred_element_type=F32)
        for p in range(T // 2):
            for e in range(2):
                half[n, p * 2 + e] = res[p * 64 : (p + 1) * 64, e * 128 : (e + 1) * 128].reshape(4, 2, 8, 128)
        k = PLACE[n]
        if KINDS[n] == "x":
            send("xa", k, half.at[n, :, far, 0], xa.at[k, 0], right)
            send("xa", k, half.at[n, :, far, 1], xa.at[k, 1], left)
        else:
            send("za", k, half.at[n, :, :, 1 - zl], za.at[k], zmate)

    def stage_two(n):
        k = PLACE[n]
        arrived("xa" if KINDS[n] == "x" else "za", k)
        if KINDS[n] == "x":
            half[n, :, xs[1], 0] += xa[k, 0]
            half[n, :, xs[3], 1] += xa[k, 1]
            send("xb", k, half.at[n, :, xs[1]], xb.at[k, 0], right)
            send("xb", k, half.at[n, :, xs[3]], xb.at[k, 1], left)
        else:
            zr[k] = half[n, :, :, zl] + za[k]
            for d in (2, 1, 3):
                send("zc", k, zr.at[k, :, xs[d]], zc.at[k, d - 1], at(xs[d], zl))

    def stage_three(n):
        k = PLACE[n]
        arrived("xb", k)
        xr[k] = half[n, :, x] + xb[k, 0] + xb[k, 1]
        send("zs", k, xr.at[k, :, 1 - zl], zs.at[k], zmate)

    def stage_four(n):
        k = PLACE[n]
        arrived("zs" if KINDS[n] == "x" else "zc", k)
        if KINDS[n] == "x":
            value = xr[k, :, zl] + zs[k]
        else:
            value = zr[k, :, x] + zc[k, 0] + zc[k, 1] + zc[k, 2]
        fin[n] = value.reshape(T * 8, 128)
        for s in range(8):
            parts[n, s] = fin[n, pl.ds(s, T, stride=8), :]
        h_ref[sample, pl.ds(n * T, T)] = parts[n, sample]
        for d in (5, 4, 3, 6, 2, 7, 1):
            send("h", 0, parts.at[n, samples[d]], h_ref.at[sample, pl.ds(n * T, T)], mates[d])

    def second_block(d):
        columns = pl.ds(pl.multiple_of(xs[d] * 256, 256), 256)
        s2[d] = lax.dot_general(
            xv[:, :, columns].reshape(48 * 64, 256), krao[...],
            (((0,), (0,)), ((), ())), preferred_element_type=F32,
        ).reshape(2, 2, 4, 16, 256)
        send("sc", d, s2.at[d, :, 1 - c], s2_in.at[d], mate)

    def second_one(d):
        arrived("sc", d)
        s2_in[d] += s2[d, :, c]
        for e in (2, 1, 3):
            send("sy", d, s2_in.at[d, :, ys[e]], s2_y.at[d, e - 1], (space, ys[e] * 2 + zh))

    def second_two(d):
        arrived("sy", d)
        total = s2_in[d, :, y] + s2_y[d, 0] + s2_y[d, 1] + s2_y[d, 2]
        s2_r[d] = total.reshape(2, 2, 8, 256)
        for way in around:
            if way[0] == d:
                _, e, f = way
                send(
                    "sz", 0, s2_r.at[d, 1 - zl if e else zl, 1 - zh if f else zh],
                    s2_z.at[d * 4 + e * 2 + f], spread(*way),
                )

    def points(n, first):
        block = xv[pl.ds(n * T, T)].reshape(rows_in, 1024)
        third = three_ref[n * T : (n + 1) * T, :].astype(F32)
        proj = jnp.dot(block, two[...], preferred_element_type=F32).reshape(T, 64, 256)
        q = jnp.sum(proj * one[None], axis=1)
        q_own[0, pl.ds(n * T, T)] = q[:, :128]
        q_own[1, pl.ds(n * T, T)] = q[:, 128:]
        return first + jnp.sum(proj * third[:, None, :], axis=0)

    def q_one():
        send("qc", 0, q_own.at[1 - c], q_in, mate)

    def q_two():
        arrived("qc")
        total = q_in[...] + q_own[c]
        mine3 = jnp.where(c == 0, three_ref[:, :128], three_ref[:, 128:]).astype(F32)
        mine4 = jnp.where(c == 0, four[:, :128], four[:, 128:])
        q_a[pl.ds(0, 48)] = total * mine4
        q_a[pl.ds(48, 8)] = jnp.broadcast_to(jnp.sum(total * mine3, axis=0, keepdims=True), (8, 128))
        for d in (2, 1, 3):
            send("qx", 0, q_a, q_x.at[d - 1], at(xs[d], zl))

    def q_three():
        arrived("qx")
        q_b[...] = q_a[...] + q_x[0] + q_x[1] + q_x[2]
        for d in (2, 1, 3):
            send("qy", 0, q_b.at[pl.ds(0, 48)], q_y.at[d - 1], (space, ys[d] * 2 + zh))

    def q_four():
        arrived("qy")
        q_s[0, pl.ds(0, 48)] = q_b[pl.ds(0, 48)] + q_y[0] + q_y[1] + q_y[2]
        q_s[0, pl.ds(48, 8)] = q_b[pl.ds(48, 8)]
        for e, f in ((0, 1), (1, 1), (1, 0), (0, 0)):
            slot = e * 2 + f
            px, py = spread(0, e, f)
            send("qz", 0, q_s.at[0], q_s.at[4 + slot], (px + 1 - 2 * c, py))
            if slot:
                send("qz", 0, q_s.at[0], q_s.at[slot], (px, py))

    def one_sends():
        for d in range(1, 8):
            rows = pl.ds(pl.multiple_of(samples[d] * 32, 32), 32)
            send("one", 0, s1_own.at[rows], s1_in.at[d - 1], mates[d])

    project(0)
    load_cone.wait()
    own = cone[pl.ds(pl.multiple_of(space * 64, 64), 64), :]
    other = cone[pl.ds(pl.multiple_of((x * 4 + zl * 2 + 1 - c) * 64, 64), 64), :]
    weight[0:64, 0:128] = own
    weight[64:128, 128:256] = own
    weight[128:192, 0:128] = other
    weight[192:256, 128:256] = other
    first = jnp.zeros((64, 256), F32)
    project(1)
    project(2)
    contract(0)
    project(3)
    contract(1)
    project(4)
    contract(2)
    project(5)
    contract(3)
    contract(4)
    load_two.wait()
    for n in range(0, 3):
        first = points(n, first)
    stage_two(1)
    contract(5)
    stage_two(0)
    for n in range(3, CHUNKS):
        first = points(n, first)
    q_one()
    stage_two(2)
    stage_two(4)
    second_block(2)
    q_two()
    second_block(1)
    second_one(2)
    stage_three(1)
    stage_two(3)
    second_block(3)
    second_one(1)
    stage_three(2)
    second_block(0)
    stage_two(5)
    q_three()
    s1_own[...] = jnp.zeros_like(s1_own)
    s1_own[:, :64] = (first * four).T
    second_one(3)
    stage_four(1)
    second_one(0)
    one_sends()
    stage_three(4)
    second_two(2)
    second_two(1)
    q_four()
    stage_four(0)
    stage_four(2)
    second_two(3)
    stage_four(4)
    stage_four(3)
    second_two(0)
    stage_four(5)

    arrived("one")
    total = s1_own[pl.ds(pl.multiple_of(sample * 32, 32), 32)]
    for d in range(1, 8):
        total = total + s1_in[d - 1]
    o1_ref[...] = total[:, :64]

    arrived("qz")
    here = q_s[0, pl.ds(0, 48)] + q_s[1, pl.ds(0, 48)] + q_s[2, pl.ds(0, 48)] + q_s[3, pl.ds(0, 48)]
    there = q_s[4, pl.ds(0, 48)] + q_s[5, pl.ds(0, 48)] + q_s[6, pl.ds(0, 48)] + q_s[7, pl.ds(0, 48)]
    low = jnp.where(c == 0, here, there)
    top = jnp.where(c == 0, there, here)
    o3_ref[:, :128] = low
    o3_ref[:, 128:] = top
    here = q_s[0, pl.ds(48, 1)] + q_s[2, pl.ds(48, 1)]
    there = q_s[4, pl.ds(48, 1)] + q_s[6, pl.ds(48, 1)]
    o4_ref[:, :128] = jnp.where(c == 0, here, there)
    o4_ref[:, 128:] = jnp.where(c == 0, there, here)

    arrived("sz")
    total = s2_r[0, zl, zh]
    for d in range(1, 16):
        total = total + s2_z[d]
    o2_ref[...] = total
    arrived("h")
    for copy in late:
        copy.wait()
    for kind in order:
        sent(kind)


def fused(ensemble, map_one, map_two, map_three, map_four, core_one, core_two, core_three, core_four):
    k = CHUNKS // 2
    vmem = lambda *shape: pltpu.VMEM(shape, F32)
    there = pl.BlockSpec(memory_space=pl.ANY)
    return pl.pallas_call(
        fused_kernel,
        in_specs=[there] * 9,
        out_specs=[pl.BlockSpec(memory_space=pltpu.VMEM)] * 7,
        out_shape=[
            pltpu.VMEM((8, 48, 128), F32),
            pltpu.VMEM((32, 64), F32),
            pltpu.VMEM((8, 256), F32),
            pltpu.VMEM((48, 256), F32),
            pltpu.VMEM((1, 256), F32),
            pltpu.VMEM((48, 128), BF16),
            pltpu.VMEM((8, 128), BF16),
        ],
        scratch_shapes=[
            pltpu.VMEM((64, 256), BF16),
            pltpu.VMEM((48, 256), BF16),
            pltpu.VMEM((1, 256), BF16),
            pltpu.VMEM((48, 64, 1024), BF16),
            pltpu.VMEM((1024, 256), BF16),
            pltpu.VMEM((1024, 128), BF16),
            pltpu.VMEM((128, 1024), BF16),
            pltpu.VMEM((1024, 128), BF16),
            pltpu.VMEM((48 * 64, 256), BF16),
            vmem(2, 8, 8, 3072),
            pltpu.VMEM((256, 256), BF16),
            vmem(8, 8, 3072),
            vmem(CHUNKS, T, 4, 2, 8, 128),
            vmem(k, 2, T, 8, 128),
            vmem(k, 2, T, 2, 8, 128),
            vmem(k, T, 2, 8, 128),
            vmem(k, T, 4, 8, 128),
            vmem(k, T, 4, 8, 128),
            vmem(k, T, 8, 128),
            vmem(k, 3, T, 8, 128),
            vmem(CHUNKS, T * 8, 128),
            vmem(CHUNKS, 8, T, 128),
            vmem(2, 48, 128),
            vmem(48, 128),
            vmem(56, 128),
            vmem(3, 56, 128),
            vmem(56, 128),
            vmem(3, 48, 128),
            vmem(8, 56, 128),
            vmem(256, 128),
            vmem(7, 32, 128),
            vmem(4, 2, 2, 4, 16, 256),
            vmem(4, 2, 4, 16, 256),
            vmem(4, 3, 2, 16, 256),
            vmem(4, 2, 2, 8, 256),
            vmem(16, 8, 256),
            pltpu.SemaphoreType.DMA((CHUNKS + 8,)),
            pltpu.SemaphoreType.DMA((15,)),
            pltpu.SemaphoreType.DMA((36,)),
        ],
        compiler_params=pltpu.CompilerParams(collective_id=0, has_side_effects=True),
        name="sketch_and_exchange",
    )(ensemble, map_two, core_two, core_one, map_one, map_three, map_four, core_three, core_four)


def final_kernel(
    h_ref, i1_ref, i2_ref, i3_ref, i4_ref, three_ref, four_ref,
    out_ref, o1_ref, o2_ref, o3_ref, o4_ref,
    grown, lhs, blocks, result, sem,
):
    passed = [(i1_ref, o1_ref), (i2_ref, o2_ref), (i3_ref, o3_ref), (i4_ref, o4_ref)]
    passes = [pltpu.make_async_copy(src, dst, sem.at[8 + n]) for n, (src, dst) in enumerate(passed)]
    for copy in passes:
        copy.start()
    four = jnp.tile(four_ref[...].astype(F32), (16, 2))
    row = lax.broadcasted_iota(jnp.int32, (128, 256), 0) // 8
    col = lax.broadcasted_iota(jnp.int32, (128, 256), 1) // 128
    for j in range(8):
        part = jnp.where(row == col + 2 * j, four, 0.0).astype(BF16)
        blocks[j, 0:128] = part
        blocks[j, 128:256] = part
    three = three_ref[...]
    three = jnp.concatenate([three, three], axis=0)
    for s in range(8):
        high, low = two_terms(h_ref[s])
        both = jnp.concatenate([high, low], axis=0)
        grown[pl.ds(s, 128, stride=8), :] = lax.dot_general(
            both, three, (((0,), (0,)), ((), ())), preferred_element_type=F32
        )
    for i in range(8):
        high, low = two_terms(grown[pl.ds(i * 128, 128), :].T)
        lhs[i * 128 : (i + 1) * 128, 0:128] = high
        lhs[i * 128 : (i + 1) * 128, 128:256] = low
    writes = []
    for j in range(8):
        res = jnp.dot(lhs[...], blocks[j], preferred_element_type=F32)
        for e in range(2):
            result[j, :, e] = res[:, e * 128 : (e + 1) * 128].reshape(8, 128, 128)
        copy = pltpu.make_async_copy(result.at[j], out_ref.at[:, j], sem.at[j])
        copy.start()
        writes.append(copy)
    for copy in writes + passes:
        copy.wait()


def final(*kept):
    here = pl.BlockSpec(memory_space=pltpu.VMEM)
    there = pl.BlockSpec(memory_space=pl.ANY)
    return pl.pallas_call(
        final_kernel,
        in_specs=[here] * 7,
        out_specs=[there] * 5,
        out_shape=[
            jax.ShapeDtypeStruct((8, 8, 2, 128, 128), F32),
            jax.ShapeDtypeStruct((32, 64), F32),
            jax.ShapeDtypeStruct((8, 256), F32),
            jax.ShapeDtypeStruct((48, 256), F32),
            jax.ShapeDtypeStruct((1, 256), F32),
        ],
        scratch_shapes=[
            pltpu.VMEM((1024, 128), F32),
            pltpu.VMEM((1024, 256), BF16),
            pltpu.VMEM((8, 256, 256), BF16),
            pltpu.VMEM((8, 8, 2, 128, 128), F32),
            pltpu.SemaphoreType.DMA((12,)),
        ],
        name="final",
    )(*kept)


def on_device(
    ensemble, map_one, map_two, map_three, map_four, core_one, core_two, core_three, core_four
):
    kept = fused(
        ensemble, map_one, map_two, map_three, map_four, core_one, core_two, core_three, core_four
    )
    kept = [pltpu.with_memory_space_constraint(value, pltpu.VMEM) for value in kept]
    core, s1, s2, s3, s4 = final(*kept)
    return (s1.T, s2, s3, s4, core.reshape(128, 128, 128))


def solution(mesh):
    placed = (
        P(None, "sample", "space", None),
        P("space", None),
        P(),
        P(),
        P("sample", None),
        P(),
        P(),
        P(),
        P(),
    )
    return jax.shard_map(
        on_device,
        mesh=mesh,
        in_specs=placed,
        out_specs=(
            P("space", "sample"),
            P(("space", "sample"), None),
            P(),
            P("sample", None),
            P(None, ("space", "sample"), None),
        ),
        check_vma=False,
    )
```

```python
import jax
import jax.numpy as jnp
from jax import lax
from jax.experimental import pallas as pl
from jax.experimental.pallas import tpu as pltpu
from jax.sharding import PartitionSpec as P

F32 = jnp.float32
BF16 = jnp.bfloat16
MESH = pl.DeviceIdType.MESH
T = 8


def two_terms(value):
    high = value.astype(BF16)
    low = (value - high.astype(F32)).astype(BF16)
    return high, low


CHUNKS = 6
KINDS = "zxxzxz"
PLACE = (0, 0, 1, 1, 2, 2)


def fused_kernel(
    ens_ref, two_ref, ctwo_ref, cone_ref, one_hbm, three_hbm, four_hbm, cthree_hbm, cfour_hbm,
    h_ref, o1_ref, o2_ref, o3_ref, o4_ref, cthree_ref, cfour_ref,
    one_ref, three_ref, four_ref,
    xv, two, ctwo, turned, cone, krao, cp, weight, cp_in, half, xa, xb, xr, za, zr, zs, zc, fin, parts,
    q_own, q_in, q_a, q_x, q_b, q_y, q_s, s1_own, s1_in,
    s2, s2_in, s2_y, s2_r, s2_z,
    load_sem, send_sem, recv_sem,
):
    space = lax.axis_index("space")
    sample = lax.axis_index("sample")
    x, zl, c = space // 4, (space // 2) % 2, space % 2
    y, zh = sample // 2, sample % 2
    xs = [lax.rem(x + d, 4) for d in range(4)]
    ys = [lax.rem(y + d, 4) for d in range(4)]
    samples = [lax.rem(sample + d, 8) for d in range(8)]
    at = lambda px, pz: (px * 4 + pz * 2 + c, sample)
    mate = (x * 4 + zl * 2 + (1 - c), sample)
    zmate = at(x, 1 - zl)
    right, left = at(xs[1], zl), at(xs[3], zl)
    mates = [(space, samples[d]) for d in range(8)]

    barrier = pltpu.get_barrier_semaphore()
    spread = lambda d, e, f: (xs[d] * 4 + (1 - zl if e else zl) * 2 + c, y * 2 + (1 - zh if f else zh))
    around = [(d, e, f) for d in (2, 1, 3, 0) for e in (1, 0) for f in (1, 0) if (d, e, f) != (0, 0, 0)]
    peers = [mate] + [spread(*way) for way in around] + [(space, ys[d] * 2 + zh) for d in (1, 2, 3)]
    peers += [(space, ys[d] * 2 + 1 - zh) for d in (1, 2, 3)]
    peers += [(spread(0, e, f)[0] + 1 - 2 * c, spread(0, e, f)[1]) for e, f in ((0, 1), (1, 0), (1, 1))]
    for peer in peers:
        pl.semaphore_signal(barrier, inc=1, device_id=peer, device_id_type=MESH)

    def load(src, dst, slot):
        copy = pltpu.make_async_copy(src, dst, load_sem.at[slot])
        copy.start()
        return copy

    load_ctwo = load(ctwo_ref, ctwo, CHUNKS)
    loads = [load(ens_ref.at[pl.ds(0, T), 0], xv.at[pl.ds(0, T)], 0)]
    small = [
        load(one_hbm, one_ref, CHUNKS + 3),
        load(three_hbm, three_ref, CHUNKS + 4),
        load(four_hbm, four_ref, CHUNKS + 5),
    ]
    load_cone = load(cone_ref, cone, CHUNKS + 1)
    loads += [load(ens_ref.at[pl.ds(n * T, T), 0], xv.at[pl.ds(n * T, T)], n) for n in range(1, CHUNKS)]
    load_two = load(two_ref, two, CHUNKS + 2)
    late = [load(cthree_hbm, cthree_ref, CHUNKS + 6), load(cfour_hbm, cfour_ref, CHUNKS + 7)]
    weight[...] = jnp.zeros_like(weight)

    chunk_lanes = lambda n: pl.ds(n * T * 64, T * 64)
    k = CHUNKS // 2
    kinds = {
        "core": (CHUNKS, lambda n: cp_in.at[:, :, chunk_lanes(n)], cp_in),
        "xa": (k, lambda n: xa.at[n], xa),
        "xb": (k, lambda n: xb.at[n], xb),
        "za": (k, lambda n: za.at[n], za),
        "zs": (k, lambda n: zs.at[n], zs),
        "zc": (k, lambda n: zc.at[n], zc),
        "h": (1, None, h_ref.at[pl.ds(0, 7)]),
        "sc": (4, lambda n: s2_in.at[n], s2_in),
        "sy": (4, lambda n: s2_y.at[n], s2_y),
        "sz": (1, None, s2_z.at[pl.ds(1, 15)]),
        "qc": (1, None, q_in),
        "qx": (1, None, q_x),
        "qy": (1, None, q_y),
        "qz": (1, None, q_s.at[pl.ds(1, 7)]),
        "one": (1, None, s1_in),
    }
    base, total_slots = {}, 0
    for kind, (count, _, _) in kinds.items():
        base[kind] = total_slots
        total_slots += count
    order = list(kinds)

    def send(kind, n, src, dst, to):
        pltpu.make_async_remote_copy(
            src_ref=src, dst_ref=dst, send_sem=send_sem.at[order.index(kind)], recv_sem=recv_sem.at[base[kind] + n],
            device_id=to, device_id_type=MESH,
        ).start()

    def arrived(kind, n=0):
        count, part, whole = kinds[kind]
        ref = whole if part is None else part(n)
        pltpu.make_async_copy(ref, ref, recv_sem.at[base[kind] + n]).wait()

    def sent(kind):
        ref = kinds[kind][2]
        pltpu.make_async_copy(ref, ref, send_sem.at[order.index(kind)]).wait()

    far = xs[2]
    rows_in = T * 64

    load_ctwo.wait()
    turned[...] = ctwo[...].T
    for copy in small:
        copy.wait()
    one = one_ref[...].astype(F32)
    four = four_ref[...].astype(F32)

    def project(n):
        loads[n].wait()
        block = xv[pl.ds(n * T, T)].reshape(rows_in, 1024)
        value = lax.dot_general(
            turned[...], block, (((1,), (1,)), ((), ())), preferred_element_type=F32
        ).reshape(8, 2, 8, rows_in)
        lanes = pl.ds(n * rows_in, rows_in)
        for e in range(2):
            cp[e, :, :, lanes] = value[:, e]
        if n == 0:
            pl.semaphore_wait(barrier, len(peers))
        send("core", n, cp.at[1 - c, :, :, lanes], cp_in.at[:, :, lanes], mate)
        third = three_ref[n * T : (n + 1) * T, :].astype(F32)
        krao[n * rows_in : (n + 1) * rows_in, :] = (
            ((third * four)[:, None, :] * one[None]).astype(BF16).reshape(rows_in, 256)
        )

    def contract(n):
        arrived("core", n)
        rows = []
        for p in range(T // 2):
            lanes = pl.ds(n * rows_in + p * 128, 128)
            mine = cp[c, :, :, lanes].reshape(64, 128)
            theirs = cp_in[:, :, lanes].reshape(64, 128)
            rows.append(jnp.concatenate([mine, theirs], axis=1))
        high, low = two_terms(jnp.concatenate(rows, axis=0))
        res = jnp.dot(high, weight[...], preferred_element_type=F32)
        res = res + jnp.dot(low, weight[...], preferred_element_type=F32)
        for p in range(T // 2):
            for e in range(2):
                half[n, p * 2 + e] = res[p * 64 : (p + 1) * 64, e * 128 : (e + 1) * 128].reshape(4, 2, 8, 128)
        k = PLACE[n]
        if KINDS[n] == "x":
            send("xa", k, half.at[n, :, far, 0], xa.at[k, 0], right)
            send("xa", k, half.at[n, :, far, 1], xa.at[k, 1], left)
        else:
            send("za", k, half.at[n, :, :, 1 - zl], za.at[k], zmate)

    def stage_two(n):
        k = PLACE[n]
        arrived("xa" if KINDS[n] == "x" else "za", k)
        if KINDS[n] == "x":
            half[n, :, xs[1], 0] += xa[k, 0]
            half[n, :, xs[3], 1] += xa[k, 1]
            send("xb", k, half.at[n, :, xs[1]], xb.at[k, 0], right)
            send("xb", k, half.at[n, :, xs[3]], xb.at[k, 1], left)
        else:
            zr[k] = half[n, :, :, zl] + za[k]
            for d in (2, 1, 3):
                send("zc", k, zr.at[k, :, xs[d]], zc.at[k, d - 1], at(xs[d], zl))

    def stage_three(n):
        k = PLACE[n]
        arrived("xb", k)
        xr[k] = half[n, :, x] + xb[k, 0] + xb[k, 1]
        send("zs", k, xr.at[k, :, 1 - zl], zs.at[k], zmate)

    def stage_four(n):
        k = PLACE[n]
        arrived("zs" if KINDS[n] == "x" else "zc", k)
        if KINDS[n] == "x":
            value = xr[k, :, zl] + zs[k]
        else:
            value = zr[k, :, x] + zc[k, 0] + zc[k, 1] + zc[k, 2]
        fin[n] = value.reshape(T * 8, 128)
        for s in range(8):
            parts[n, s] = fin[n, pl.ds(s, T, stride=8), :]
        h_ref[sample, pl.ds(n * T, T)] = parts[n, sample]
        for d in (5, 4, 3, 6, 2, 7, 1):
            send("h", 0, parts.at[n, samples[d]], h_ref.at[sample, pl.ds(n * T, T)], mates[d])

    def second_block(d):
        columns = pl.ds(pl.multiple_of(xs[d] * 256, 256), 256)
        s2[d] = lax.dot_general(
            xv[:, :, columns].reshape(48 * 64, 256), krao[...],
            (((0,), (0,)), ((), ())), preferred_element_type=F32,
        ).reshape(2, 2, 4, 16, 256)
        send("sc", d, s2.at[d, :, 1 - c], s2_in.at[d], mate)

    def second_one(d):
        arrived("sc", d)
        s2_in[d] += s2[d, :, c]
        for e in (2, 1, 3):
            send("sy", d, s2_in.at[d, :, ys[e]], s2_y.at[d, e - 1], (space, ys[e] * 2 + zh))

    def second_two(d):
        arrived("sy", d)
        total = s2_in[d, :, y] + s2_y[d, 0] + s2_y[d, 1] + s2_y[d, 2]
        s2_r[d] = total.reshape(2, 2, 8, 256)
        for way in around:
            if way[0] == d:
                _, e, f = way
                send(
                    "sz", 0, s2_r.at[d, 1 - zl if e else zl, 1 - zh if f else zh],
                    s2_z.at[d * 4 + e * 2 + f], spread(*way),
                )

    def points(n, first):
        block = xv[pl.ds(n * T, T)].reshape(rows_in, 1024)
        third = three_ref[n * T : (n + 1) * T, :].astype(F32)
        proj = jnp.dot(block, two[...], preferred_element_type=F32).reshape(T, 64, 256)
        q = jnp.sum(proj * one[None], axis=1)
        q_own[0, pl.ds(n * T, T)] = q[:, :128]
        q_own[1, pl.ds(n * T, T)] = q[:, 128:]
        return first + jnp.sum(proj * third[:, None, :], axis=0)

    def q_one():
        send("qc", 0, q_own.at[1 - c], q_in, mate)

    def q_two():
        arrived("qc")
        total = q_in[...] + q_own[c]
        mine3 = jnp.where(c == 0, three_ref[:, :128], three_ref[:, 128:]).astype(F32)
        mine4 = jnp.where(c == 0, four[:, :128], four[:, 128:])
        q_a[pl.ds(0, 48)] = total * mine4
        q_a[pl.ds(48, 8)] = jnp.broadcast_to(jnp.sum(total * mine3, axis=0, keepdims=True), (8, 128))
        for d in (2, 1, 3):
            send("qx", 0, q_a, q_x.at[d - 1], at(xs[d], zl))

    def q_three():
        arrived("qx")
        q_b[...] = q_a[...] + q_x[0] + q_x[1] + q_x[2]
        for d in (2, 1, 3):
            send("qy", 0, q_b.at[pl.ds(0, 48)], q_y.at[d - 1], (space, ys[d] * 2 + zh))

    def q_four():
        arrived("qy")
        q_s[0, pl.ds(0, 48)] = q_b[pl.ds(0, 48)] + q_y[0] + q_y[1] + q_y[2]
        q_s[0, pl.ds(48, 8)] = q_b[pl.ds(48, 8)]
        for e, f in ((0, 1), (1, 1), (1, 0), (0, 0)):
            slot = e * 2 + f
            px, py = spread(0, e, f)
            send("qz", 0, q_s.at[0], q_s.at[4 + slot], (px + 1 - 2 * c, py))
            if slot:
                send("qz", 0, q_s.at[0], q_s.at[slot], (px, py))

    def one_sends():
        for d in range(1, 8):
            rows = pl.ds(pl.multiple_of(samples[d] * 32, 32), 32)
            send("one", 0, s1_own.at[rows], s1_in.at[d - 1], mates[d])

    project(0)
    load_cone.wait()
    own = cone[pl.ds(pl.multiple_of(space * 64, 64), 64), :]
    other = cone[pl.ds(pl.multiple_of((x * 4 + zl * 2 + 1 - c) * 64, 64), 64), :]
    weight[0:64, 0:128] = own
    weight[64:128, 128:256] = own
    weight[128:192, 0:128] = other
    weight[192:256, 128:256] = other
    first = jnp.zeros((64, 256), F32)
    project(1)
    project(2)
    contract(0)
    project(3)
    contract(1)
    project(4)
    contract(2)
    project(5)
    contract(3)
    contract(4)
    load_two.wait()
    for n in range(0, 3):
        first = points(n, first)
    stage_two(1)
    contract(5)
    stage_two(0)
    for n in range(3, CHUNKS):
        first = points(n, first)
    q_one()
    stage_two(2)
    stage_two(4)
    second_block(2)
    q_two()
    second_block(1)
    second_one(2)
    stage_three(1)
    stage_two(3)
    second_block(3)
    second_one(1)
    stage_three(2)
    second_block(0)
    stage_two(5)
    q_three()
    s1_own[...] = jnp.zeros_like(s1_own)
    s1_own[:, :64] = (first * four).T
    second_one(3)
    stage_four(1)
    second_one(0)
    one_sends()
    stage_three(4)
    second_two(2)
    second_two(1)
    q_four()
    stage_four(0)
    stage_four(2)
    second_two(3)
    stage_four(4)
    stage_four(3)
    stage_four(5)
    second_two(0)

    arrived("one")
    total = s1_own[pl.ds(pl.multiple_of(sample * 32, 32), 32)]
    for d in range(1, 8):
        total = total + s1_in[d - 1]
    o1_ref[...] = total[:, :64]

    arrived("qz")
    here = q_s[0, pl.ds(0, 48)] + q_s[1, pl.ds(0, 48)] + q_s[2, pl.ds(0, 48)] + q_s[3, pl.ds(0, 48)]
    there = q_s[4, pl.ds(0, 48)] + q_s[5, pl.ds(0, 48)] + q_s[6, pl.ds(0, 48)] + q_s[7, pl.ds(0, 48)]
    low = jnp.where(c == 0, here, there)
    top = jnp.where(c == 0, there, here)
    o3_ref[:, :128] = low
    o3_ref[:, 128:] = top
    here = q_s[0, pl.ds(48, 1)] + q_s[2, pl.ds(48, 1)]
    there = q_s[4, pl.ds(48, 1)] + q_s[6, pl.ds(48, 1)]
    o4_ref[:, :128] = jnp.where(c == 0, here, there)
    o4_ref[:, 128:] = jnp.where(c == 0, there, here)

    arrived("sz")
    total = s2_r[0, zl, zh]
    for d in range(1, 16):
        total = total + s2_z[d]
    o2_ref[...] = total
    arrived("h")
    for copy in late:
        copy.wait()
    for kind in order:
        sent(kind)


def fused(ensemble, map_one, map_two, map_three, map_four, core_one, core_two, core_three, core_four):
    k = CHUNKS // 2
    vmem = lambda *shape: pltpu.VMEM(shape, F32)
    there = pl.BlockSpec(memory_space=pl.ANY)
    return pl.pallas_call(
        fused_kernel,
        in_specs=[there] * 9,
        out_specs=[pl.BlockSpec(memory_space=pltpu.VMEM)] * 7,
        out_shape=[
            pltpu.VMEM((8, 48, 128), F32),
            pltpu.VMEM((32, 64), F32),
            pltpu.VMEM((8, 256), F32),
            pltpu.VMEM((48, 256), F32),
            pltpu.VMEM((1, 256), F32),
            pltpu.VMEM((48, 128), BF16),
            pltpu.VMEM((8, 128), BF16),
        ],
        scratch_shapes=[
            pltpu.VMEM((64, 256), BF16),
            pltpu.VMEM((48, 256), BF16),
            pltpu.VMEM((1, 256), BF16),
            pltpu.VMEM((48, 64, 1024), BF16),
            pltpu.VMEM((1024, 256), BF16),
            pltpu.VMEM((1024, 128), BF16),
            pltpu.VMEM((128, 1024), BF16),
            pltpu.VMEM((1024, 128), BF16),
            pltpu.VMEM((48 * 64, 256), BF16),
            vmem(2, 8, 8, 3072),
            pltpu.VMEM((256, 256), BF16),
            vmem(8, 8, 3072),
            vmem(CHUNKS, T, 4, 2, 8, 128),
            vmem(k, 2, T, 8, 128),
            vmem(k, 2, T, 2, 8, 128),
            vmem(k, T, 2, 8, 128),
            vmem(k, T, 4, 8, 128),
            vmem(k, T, 4, 8, 128),
            vmem(k, T, 8, 128),
            vmem(k, 3, T, 8, 128),
            vmem(CHUNKS, T * 8, 128),
            vmem(CHUNKS, 8, T, 128),
            vmem(2, 48, 128),
            vmem(48, 128),
            vmem(56, 128),
            vmem(3, 56, 128),
            vmem(56, 128),
            vmem(3, 48, 128),
            vmem(8, 56, 128),
            vmem(256, 128),
            vmem(7, 32, 128),
            vmem(4, 2, 2, 4, 16, 256),
            vmem(4, 2, 4, 16, 256),
            vmem(4, 3, 2, 16, 256),
            vmem(4, 2, 2, 8, 256),
            vmem(16, 8, 256),
            pltpu.SemaphoreType.DMA((CHUNKS + 8,)),
            pltpu.SemaphoreType.DMA((15,)),
            pltpu.SemaphoreType.DMA((36,)),
        ],
        compiler_params=pltpu.CompilerParams(collective_id=0, has_side_effects=True),
        name="sketch_and_exchange",
    )(ensemble, map_two, core_two, core_one, map_one, map_three, map_four, core_three, core_four)


def final_kernel(
    h_ref, i1_ref, i2_ref, i3_ref, i4_ref, three_ref, four_ref,
    out_ref, o1_ref, o2_ref, o3_ref, o4_ref,
    grown, lhs, blocks, result, sem,
):
    passed = [(i1_ref, o1_ref), (i2_ref, o2_ref), (i3_ref, o3_ref), (i4_ref, o4_ref)]
    passes = [pltpu.make_async_copy(src, dst, sem.at[16 + n]) for n, (src, dst) in enumerate(passed)]
    for copy in passes:
        copy.start()
    four = jnp.tile(four_ref[...].astype(F32), (16, 2))
    row = lax.broadcasted_iota(jnp.int32, (128, 256), 0) // 8
    col = lax.broadcasted_iota(jnp.int32, (128, 256), 1) // 128
    for j in range(8):
        part = jnp.where(row == col + 2 * j, four, 0.0).astype(BF16)
        blocks[j, 0:128] = part
        blocks[j, 128:256] = part
    three = three_ref[...]
    three = jnp.concatenate([three, three], axis=0)
    for s in range(8):
        high, low = two_terms(h_ref[s])
        both = jnp.concatenate([high, low], axis=0)
        grown[pl.ds(s, 128, stride=8), :] = lax.dot_general(
            both, three, (((0,), (0,)), ((), ())), preferred_element_type=F32
        )
    writes = []
    for part in range(2):
        tiles = pl.ds(part * 4, 4)
        for i in range(part * 4, part * 4 + 4):
            high, low = two_terms(grown[pl.ds(i * 128, 128), :].T)
            lhs[i * 128 : (i + 1) * 128, 0:128] = high
            lhs[i * 128 : (i + 1) * 128, 128:256] = low
        for j in range(8):
            res = jnp.dot(lhs[pl.ds(part * 512, 512), :], blocks[j], preferred_element_type=F32)
            for e in range(2):
                result[j, tiles, e] = res[:, e * 128 : (e + 1) * 128].reshape(4, 128, 128)
            copy = pltpu.make_async_copy(result.at[j, tiles], out_ref.at[tiles, j], sem.at[part * 8 + j])
            copy.start()
            writes.append(copy)
    for copy in writes + passes:
        copy.wait()


def final(*kept):
    here = pl.BlockSpec(memory_space=pltpu.VMEM)
    there = pl.BlockSpec(memory_space=pl.ANY)
    return pl.pallas_call(
        final_kernel,
        in_specs=[here] * 7,
        out_specs=[there] * 5,
        out_shape=[
            jax.ShapeDtypeStruct((8, 8, 2, 128, 128), F32),
            jax.ShapeDtypeStruct((32, 64), F32),
            jax.ShapeDtypeStruct((8, 256), F32),
            jax.ShapeDtypeStruct((48, 256), F32),
            jax.ShapeDtypeStruct((1, 256), F32),
        ],
        scratch_shapes=[
            pltpu.VMEM((1024, 128), F32),
            pltpu.VMEM((1024, 256), BF16),
            pltpu.VMEM((8, 256, 256), BF16),
            pltpu.VMEM((8, 8, 2, 128, 128), F32),
            pltpu.SemaphoreType.DMA((20,)),
        ],
        name="final",
    )(*kept)


def on_device(
    ensemble, map_one, map_two, map_three, map_four, core_one, core_two, core_three, core_four
):
    kept = fused(
        ensemble, map_one, map_two, map_three, map_four, core_one, core_two, core_three, core_four
    )
    kept = [pltpu.with_memory_space_constraint(value, pltpu.VMEM) for value in kept]
    core, s1, s2, s3, s4 = final(*kept)
    return (s1.T, s2, s3, s4, core.reshape(128, 128, 128))


def solution(mesh):
    placed = (
        P(None, "sample", "space", None),
        P("space", None),
        P(),
        P(),
        P("sample", None),
        P(),
        P(),
        P(),
        P(),
    )
    return jax.shard_map(
        on_device,
        mesh=mesh,
        in_specs=placed,
        out_specs=(
            P("space", "sample"),
            P(("space", "sample"), None),
            P(),
            P("sample", None),
            P(None, ("space", "sample"), None),
        ),
        check_vma=False,
    )
```
